512 devices in a mesh: gx: 8 (over z), gy: 8 (over x, core), gz: 8 (over y).
Axes of the slice: x: 4, y: 8, z: 8, core: 2. Of those that a mesh axis runs over, the one named last changes fastest.
Arguments:
- phase_mask: int32 [128, 256, 1024], P('gx', 'gy', 'gz'), may hold values from 0 to 2
- pressure: float32 [128, 256, 1024], P('gx', 'gy', 'gz'), may hold values from -6 to 6
- velocity_cot: float32 [3, 128, 256, 1024], P(None, 'gx', 'gy', 'gz'), may hold values from -30 to 30
Outputs:
- ustar_cot: float32 [3, 128, 256, 1024], P(None, 'gx', 'gy', 'gz')
- coef_cot: float32 [128, 256, 1024], P('gx', 'gy', 'gz')
The draws below stay inside these ranges and needn't reach their ends.
Inputs may be any that keep to these rules, and one draw needn't show every extreme that they name: `phase_mask`: 0 air, 1 water, 2 interface band.
All inputs are finite; a program needn't handle non-finite values.
Results may differ from the reference program's by a relative error of at most 0.0001.
Values sent between devices are 32-bit elements; how exact they have to be, the bound alone decides.
A program may use at most 64 MiB of HBM per device.

```python
import math
import jax
import jax.numpy as jnp
from jax import lax

ITERS = 3
NX = 128
NY = 256
NZ = 1024


def draw_velocity_cot(key, part):
    shape = (3, NX, NY, NZ)
    frac_x = lax.broadcasted_iota(jnp.float32, shape, 1) / NX
    frac_y = lax.broadcasted_iota(jnp.float32, shape, 2) / NY
    frac_z = lax.broadcasted_iota(jnp.float32, shape, 3) / NZ
    scale = jnp.exp(math.log(3.0) * (frac_x + frac_y + frac_z - 1.5))
    base = jnp.clip(jax.random.normal(key, shape, jnp.float32), -5.0, 5.0)
    return (base * scale).astype(jnp.float32)


def touch_ends(values, key, low, top_value):
    spot = [jax.random.randint(jax.random.fold_in(key, axis), (), 0, length) for axis, length in enumerate(values.shape)]
    widest = values.shape.index(max(values.shape))
    beside = spot[:widest] + [(spot[widest] + 1) % values.shape[widest]] + spot[widest + 1:]
    return values.at[tuple(spot)].set(low).at[tuple(beside)].set(top_value)


def block_levels(own_key, shape, pieces, smallest, high):
    def one(position, parts):
        draws = jax.random.uniform(jax.random.fold_in(jax.random.fold_in(own_key, 6), position), (parts,), jnp.float32, smallest / len(pieces), high / len(pieces))
        return jnp.repeat(jnp.exp(draws), shape[position] // parts).reshape((-1,) + (1,) * (len(shape) - position - 1))

    level = one(*pieces[0])
    for cut in pieces[1:]:
        level = level * one(*cut)
    return level


def gaussian(own_key, shape, scale, limit, split=(), held_as=jnp.bfloat16):
    values = scale * jax.random.normal(own_key, shape, jnp.float32)
    if split:
        values = values * block_levels(own_key, shape, split, -0.22, 0.18)
    return jnp.clip(values, -limit, limit).astype(held_as)


def setup_inputs(seed: int = 0) -> dict:
    arg_keys = jax.random.split(jax.random.key(seed), 4)
    phase_mask = touch_ends(jax.random.randint(arg_keys[0], (NX, NY, NZ), 0, 3), jax.random.fold_in(arg_keys[0], 1), 0, 2).astype(jnp.int32)
    pressure = gaussian(arg_keys[1], (NX, NY, NZ), 1.0, 6.0, ((0, 8), (1, 8), (2, 8)), jnp.float32)
    velocity_cot = draw_velocity_cot(jax.random.fold_in(arg_keys[3], 71), 0)
    return dict(phase_mask=phase_mask, pressure=pressure, velocity_cot=velocity_cot)


def coefficient(phase_mask):
    return jnp.where(phase_mask == 0, 8.0, jnp.where(phase_mask == 1, 1.0, 2.0)).astype(jnp.float32)


def face_pair(padded, dim_idx):
    count = padded.shape[dim_idx]
    lower = lax.slice_in_dim(padded, 0, count - 1, axis=dim_idx)
    upper = lax.slice_in_dim(padded, 1, count, axis=dim_idx)
    for other in range(3):
        if other != dim_idx:
            width = padded.shape[other]
            lower = lax.slice_in_dim(lower, 1, width - 1, axis=other)
            upper = lax.slice_in_dim(upper, 1, width - 1, axis=other)
    return upper, lower


def face_grads(padded):
    result = []
    for dim_idx in range(3):
        upper, lower = face_pair(padded, dim_idx)
        result.append(upper - lower)
    return tuple(result)


def face_weights(coef_padded):
    result = []
    for dim_idx in range(3):
        upper, lower = face_pair(coef_padded, dim_idx)
        result.append(0.5 * (upper + lower))
    return tuple(result)


def diverge(fluxes):
    total = None
    for dim_idx in range(3):
        flux = fluxes[dim_idx]
        count = flux.shape[dim_idx]
        term = lax.slice_in_dim(flux, 0, count - 1, axis=dim_idx) - lax.slice_in_dim(flux, 1, count, axis=dim_idx)
        total = term if total is None else total + term
    return total


def spread(fluxes):
    total = None
    for dim_idx in range(3):
        flux = fluxes[dim_idx]
        count = flux.shape[dim_idx]
        term = lax.slice_in_dim(flux, 0, count - 1, axis=dim_idx) + lax.slice_in_dim(flux, 1, count, axis=dim_idx)
        total = term if total is None else total + term
    return total


def operate(padded, weights):
    grads = face_grads(padded)
    return diverge(tuple(weights[dim_idx] * grads[dim_idx] for dim_idx in range(3)))


def prepare(coef_padded, press_padded, vel_padded):
    weights = face_weights(coef_padded)
    precond = 1.0 / spread(weights)
    vel_faces = tuple(face_pair(vel_padded[dim_idx], dim_idx)[1] for dim_idx in range(3))
    rhs = -diverge(tuple(weights[dim_idx] * vel_faces[dim_idx] for dim_idx in range(3)))
    press_grads = face_grads(press_padded)
    return weights, precond, rhs, press_grads, vel_faces


def finish(lam_padded, velocity_cot, press_grads, vel_faces):
    lam_grads = face_grads(lam_padded)
    columns = []
    for dim_idx in range(3):
        count = lam_grads[dim_idx].shape[dim_idx]
        columns.append(velocity_cot[dim_idx] + lax.slice_in_dim(lam_grads[dim_idx], 1, count, axis=dim_idx))
    ustar_cot = jnp.stack(columns, 0)
    wbar = tuple(-press_grads[dim_idx] * (vel_faces[dim_idx] + lam_grads[dim_idx]) for dim_idx in range(3))
    coef_cot = 0.5 * spread(wbar)
    return ustar_cot, coef_cot


def pad_cells(field):
    return jnp.pad(field, ((1, 1), (1, 1), (1, 1)))


def reference(phase_mask, pressure, velocity_cot):
    stacked = jnp.concatenate([coefficient(phase_mask)[None], pressure[None], velocity_cot], 0)
    padded = jnp.pad(stacked, ((0, 0), (1, 1), (1, 1), (1, 1)))
    weights, precond, rhs, press_grads, vel_faces = prepare(padded[0], padded[1], padded[2:])
    solution = jnp.zeros_like(rhs)
    resid = rhs
    precd = precond * resid
    direction = precd
    rz_now = jnp.sum(resid * precd)
    for iteration in range(ITERS):
        image = operate(pad_cells(direction), weights)
        step_len = rz_now / jnp.sum(direction * image)
        solution = solution + step_len * direction
        resid = resid - step_len * image
        if iteration + 1 < ITERS:
            precd = precond * resid
            rz_next = jnp.sum(resid * precd)
            direction = precd + (rz_next / rz_now) * direction
            rz_now = rz_next
    return finish(pad_cells(solution), velocity_cot, press_grads, vel_faces)
```

```python
import jax
import jax.numpy as jnp
from jax import lax
from jax.experimental import pallas as pl
from jax.experimental.pallas import tpu as pltpu
from jax.sharding import PartitionSpec as P


MESH = pl.DeviceIdType.MESH
AXES = ("gx", "gy", "gz")
RING = 8
NXL, NYL, NZL = 16, 32, 128
TOP = 8
LAST = TOP + NYL - 1
BLOCKS = NYL // 8
F32 = jnp.float32


def two_sum(a, b):
    s = a + b
    t = s - a
    return s, (a - (s - t)) + (b - t)


def split(a):
    c = 4097.0 * a
    hi = c - (c - a)
    return hi, a - hi


def sub_mul(x, c, y):
    p = c * y[0]
    ch, cl = split(c)
    yh, yl = split(y[0])
    err = ((ch * yh - p) + ch * yl + cl * yh) + cl * yl
    s, t = two_sum(x[0], -p)
    t = t + (x[1] - (err + c * y[1]))
    hi = s + t
    return hi, t - (hi - s)


def galerkin(sums):
    g0, g2, h00, h01, h02, h11, h12, h22 = sums
    one = jnp.ones_like(g0[0])
    g1 = sub_mul(h00, one, g0)
    a = h01[0] / h00[0]
    b = h02[0] / h00[0]
    h01p = sub_mul(h01, a, h00)
    h02p = sub_mul(h02, b, h00)
    h11p = sub_mul(sub_mul(h11, a, h01), a, h01p)
    h12p = sub_mul(sub_mul(h12, a, h02), b, h01p)
    h22p = sub_mul(sub_mul(h22, b, h02), b, h02p)
    g1p = sub_mul(g1, a, g0)
    g2p = sub_mul(g2, b, g0)
    ok1 = h11p[0] > 1e-10 * h11[0]
    inv1 = jnp.where(ok1, 1.0 / jnp.where(ok1, h11p[0], 1.0), 0.0)
    c = h12p[0] * inv1
    h12q = sub_mul(h12p, c, h11p)
    h22q = sub_mul(sub_mul(h22p, c, h12p), c, h12q)
    g2q = sub_mul(g2p, c, g1p)
    h02q = h02p[0] - c * h01p[0]
    ok2 = h22q[0] > 1e-10 * h22[0]
    y2 = jnp.where(ok2, g2q[0] / jnp.where(ok2, h22q[0], 1.0), 0.0)
    y1p = (g1p[0] - h12q[0] * y2) * inv1
    y0p = (g0[0] - h01p[0] * y1p - h02q * y2) / h00[0]
    return y0p - a * y1p - (b - c * a) * y2, y1p - c * y2, y2


def roll(x, shift, axis):
    return pltpu.roll(x, shift, axis)


def remote(src, dst, send, recv, device):
    return pltpu.make_async_remote_copy(
        src_ref=src, dst_ref=dst, send_sem=send, recv_sem=recv, device_id=device, device_id_type=MESH
    )


def body(
    mask_hbm, press_hbm, vel_hbm, ustar_hbm, coef_hbm,
    mask, fc, fp, fu0, fu1, fu2, fv0, fv1, fv2,
    wx, wyu, wyd, wzu, wzd, minv, rhs, img,
    grads, bases,
    yup, ydn, yup_in, ydn_in, vyup, vydn, vyup_in, vydn_in,
    zup, zin_lo, zin_hi, zmix, vz, vz_lo, vz_hi, vmix,
    sums, out_u, out_c,
    load_sem, store_sem,
    send1, recv1, sendv, recvv, sendr, recvr,
):
    pos = {axis: lax.axis_index(axis) for axis in AXES}
    fwd = {axis: lax.rem(pos[axis] + 1, RING) for axis in AXES}
    bwd = {axis: lax.rem(pos[axis] + RING - 1, RING) for axis in AXES}
    lane = lax.broadcasted_iota(jnp.int32, (8, NZL), 1)
    half = lane // 2
    even = lane - 2 * half == 0
    first = lane == 0
    final = lane == NZL - 1

    cells = (pl.ds(1, NXL), pl.ds(TOP, NYL))
    loads = [pltpu.make_async_copy(mask_hbm, mask, load_sem.at[0])]
    for i, field in enumerate((fu0, fu1, fu2)):
        loads.append(pltpu.make_async_copy(vel_hbm.at[i], field.at[cells], load_sem.at[1 + i]))
    loads.append(pltpu.make_async_copy(press_hbm, fp.at[cells], load_sem.at[4]))
    for load in loads:
        load.start()

    barrier = pltpu.get_barrier_semaphore()
    for axis in AXES:
        for other in (fwd[axis], bwd[axis]):
            pl.semaphore_signal(barrier, inc=1, device_id={axis: other}, device_id_type=MESH)
    for load in loads:
        load.wait()

    def pick(x, k, value, packed):
        return jnp.where(half == BLOCKS * x + k, roll(value, 2 * BLOCKS * x + 2 * k + 1, 1), packed)

    def place(x, k, mixed):
        return roll(mixed, NZL - 1 - 2 * BLOCKS * x - 2 * k, 1)

    def above(value, edge):
        return jnp.where(final, edge, roll(value, NZL - 1, 1))

    def below(value, edge):
        return jnp.where(first, edge, roll(value, 1, 1))

    zero = jnp.zeros((8, NZL), F32)

    def prepare(x, carry):
        pc, pp, pu = carry
        for k in range(BLOCKS):
            rows = pl.ds(TOP + 8 * k, 8)
            phase = mask[x, pl.ds(8 * k, 8)]
            c = jnp.where(phase == 0, 8.0, jnp.where(phase == 1, 1.0, 2.0)).astype(F32)
            fc[x + 1, rows] = c
            pc = pick(x, k, c, pc)
            pp = pick(x, k, fp[x + 1, rows], pp)
            pu = pick(x, k, fu2[x + 1, rows], pu)
            if k == 0:
                ydn[0, pl.ds(x, 1)] = c[0:1]
                ydn[1, pl.ds(x, 1)] = fp[x + 1, pl.ds(TOP, 1)]
            if k == BLOCKS - 1:
                yup[0, pl.ds(x, 1)] = c[7:8]
                yup[1, pl.ds(x, 1)] = fp[x + 1, pl.ds(LAST, 1)]
                yup[2, pl.ds(x, 1)] = fu1[x + 1, pl.ds(LAST, 1)]
        return pc, pp, pu

    pc, pp, pu = lax.fori_loop(0, NXL, prepare, (zero, zero, zero), unroll=4)
    zup[0] = pc
    zup[1] = pp
    zup[2] = pu

    pl.semaphore_wait(barrier, 6)

    inner = pl.ds(TOP, NYL)
    round1 = [
        remote(fc.at[NXL, inner], fc.at[0, inner], send1.at[0], recv1.at[0], {"gx": fwd["gx"]}),
        remote(fc.at[1, inner], fc.at[NXL + 1, inner], send1.at[1], recv1.at[1], {"gx": bwd["gx"]}),
        remote(fu0.at[NXL, inner], fu0.at[0, inner], send1.at[2], recv1.at[2], {"gx": fwd["gx"]}),
        remote(fp.at[NXL, inner], fp.at[0, inner], send1.at[3], recv1.at[3], {"gx": fwd["gx"]}),
        remote(fp.at[1, inner], fp.at[NXL + 1, inner], send1.at[4], recv1.at[4], {"gx": bwd["gx"]}),
        remote(yup, yup_in, send1.at[5], recv1.at[5], {"gy": fwd["gy"]}),
        remote(ydn, ydn_in, send1.at[6], recv1.at[6], {"gy": bwd["gy"]}),
        remote(zup, zin_lo, send1.at[7], recv1.at[7], {"gz": fwd["gz"]}),
        remote(zup, zin_hi, send1.at[8], recv1.at[8], {"gz": bwd["gz"]}),
    ]
    for copy in round1:
        copy.start()
    for copy in round1:
        copy.wait_recv()

    low = {axis: pos[axis] == 0 for axis in AXES}
    high = {axis: pos[axis] == RING - 1 for axis in AXES}

    def clear_x(fields_low, fields_high):
        @pl.when(low["gx"])
        def _():
            for field in fields_low:
                field[0, inner] = jnp.zeros((NYL, NZL), F32)

        @pl.when(high["gx"])
        def _():
            for field in fields_high:
                field[NXL + 1, inner] = jnp.zeros((NYL, NZL), F32)

    def mix(lo, hi):
        lo = jnp.where(low["gz"], 0.0, lo)
        hi = jnp.where(high["gz"], 0.0, hi)
        return jnp.where(even, roll(hi, NZL - 1, 1), roll(lo, 1, 1))

    clear_x((fc, fp, fu0), (fc, fp))
    for i in range(3):
        zmix[i] = mix(zin_lo[i], zin_hi[i])
    for x in range(NXL):
        row = pl.ds(x, 1)
        fc[x + 1, pl.ds(TOP - 1, 1)] = jnp.where(low["gy"], 0.0, yup_in[0, row])
        fp[x + 1, pl.ds(TOP - 1, 1)] = jnp.where(low["gy"], 0.0, yup_in[1, row])
        fu1[x + 1, pl.ds(TOP - 1, 1)] = jnp.where(low["gy"], 0.0, yup_in[2, row])
        fc[x + 1, pl.ds(LAST + 1, 1)] = jnp.where(high["gy"], 0.0, ydn_in[0, row])
        fp[x + 1, pl.ds(LAST + 1, 1)] = jnp.where(high["gy"], 0.0, ydn_in[1, row])

    wx[0] = 0.5 * (fc[0, inner] + fc[1, inner])

    def faces(x, k, value):
        if k == 0:
            vydn[pl.ds(x, 1)] = value[0:1]
        if k == BLOCKS - 1:
            vyup[pl.ds(x, 1)] = value[7:8]

    def start(x, carry):
        packed, g0 = carry
        for k in range(BLOCKS):
            r = TOP + 8 * k
            rows, own = pl.ds(r, 8), pl.ds(8 * k, 8)
            c = fc[x + 1, rows]
            edge = place(x, k, zmix[0])
            xu = 0.5 * (c + fc[x + 2, rows])
            xd = wx[x, own]
            yu = 0.5 * (c + fc[x + 1, pl.ds(r + 1, 8)])
            yd = 0.5 * (c + fc[x + 1, pl.ds(r - 1, 8)])
            zu = 0.5 * (c + above(c, edge))
            zd = 0.5 * (c + below(c, edge))
            m = 1.0 / ((xd + xu) + (yd + yu) + (zd + zu))
            u2 = fu2[x + 1, rows]
            r0 = (
                (xu * fu0[x + 1, rows] - xd * fu0[x, rows])
                + (yu * fu1[x + 1, rows] - yd * fu1[x + 1, pl.ds(r - 1, 8)])
                + (zu * u2 - zd * below(u2, place(x, k, zmix[2])))
            )
            v = m * r0
            wx[x + 1, own] = xu
            wyu[x, own] = yu
            wyd[x, own] = yd
            wzu[x, own] = zu
            wzd[x, own] = zd
            minv[x, own] = m
            rhs[x, own] = r0
            fv0[x + 1, rows] = v
            packed = pick(x, k, v, packed)
            faces(x, k, v)
            g0 = g0 + v * r0
        return packed, g0

    packed, g0 = lax.fori_loop(0, NXL, start, (zero, zero), unroll=4)

    def exchange(i, field, packed):
        vz[i] = packed
        copies = [
            remote(field.at[NXL, inner], field.at[0, inner], sendv.at[i, 0], recvv.at[i, 0], {"gx": fwd["gx"]}),
            remote(field.at[1, inner], field.at[NXL + 1, inner], sendv.at[i, 1], recvv.at[i, 1], {"gx": bwd["gx"]}),
            remote(vyup, vyup_in.at[i], sendv.at[i, 2], recvv.at[i, 2], {"gy": fwd["gy"]}),
            remote(vydn, vydn_in.at[i], sendv.at[i, 3], recvv.at[i, 3], {"gy": bwd["gy"]}),
            remote(vz.at[i], vz_lo.at[i], sendv.at[i, 4], recvv.at[i, 4], {"gz": fwd["gz"]}),
            remote(vz.at[i], vz_hi.at[i], sendv.at[i, 5], recvv.at[i, 5], {"gz": bwd["gz"]}),
        ]
        for copy in copies:
            copy.start()
        for copy in copies:
            copy.wait()
        clear_x((field,), (field,))
        vmix[i] = mix(vz_lo[i], vz_hi[i])
        for x in range(NXL):
            row = pl.ds(x, 1)
            field[x + 1, pl.ds(TOP - 1, 1)] = jnp.where(low["gy"], 0.0, vyup_in[i, row])
            field[x + 1, pl.ds(LAST + 1, 1)] = jnp.where(high["gy"], 0.0, vydn_in[i, row])

    def around(x, k, i, field):
        r = TOP + 8 * k
        rows = pl.ds(r, 8)
        v = field[x + 1, rows]
        edge = place(x, k, vmix[i])
        return (
            v,
            (field[x + 2, rows], field[x + 1, pl.ds(r + 1, 8)], above(v, edge)),
            (field[x, rows], field[x + 1, pl.ds(r - 1, 8)], below(v, edge)),
        )

    def operate(x, k, i, field):
        own = pl.ds(8 * k, 8)
        v, (xp, yp, zp), (xm, ym, zm) = around(x, k, i, field)
        image = (
            (wx[x, own] * (v - xm) + wx[x + 1, own] * (v - xp))
            + (wyd[x, own] * (v - ym) + wyu[x, own] * (v - yp))
            + (wzd[x, own] * (v - zm) + wzu[x, own] * (v - zp))
        )
        return v, image

    exchange(0, fv0, packed)

    def step0(x, carry):
        packed, h00, h01 = carry
        for k in range(BLOCKS):
            own = pl.ds(8 * k, 8)
            v, q = operate(x, k, 0, fv0)
            w = minv[x, own] * q - v
            img[x, own] = q
            fv1[x + 1, pl.ds(TOP + 8 * k, 8)] = w
            packed = pick(x, k, w, packed)
            faces(x, k, w)
            h00 = h00 + v * q
            h01 = h01 + w * q
        return packed, h00, h01

    packed, h00, h01 = lax.fori_loop(0, NXL, step0, (zero, zero, zero), unroll=4)
    exchange(1, fv1, packed)

    def step1(x, carry):
        packed, h02, h11, h12, g2 = carry
        for k in range(BLOCKS):
            own = pl.ds(8 * k, 8)
            v, q = operate(x, k, 1, fv1)
            w = minv[x, own] * q - v
            fv2[x + 1, pl.ds(TOP + 8 * k, 8)] = w
            packed = pick(x, k, w, packed)
            faces(x, k, w)
            h02 = h02 + w * img[x, own]
            h11 = h11 + v * q
            h12 = h12 + w * q
            g2 = g2 + w * rhs[x, own]
        return packed, h02, h11, h12, g2

    packed, h02, h11, h12, g2 = lax.fori_loop(0, NXL, step1, (zero,) * 5, unroll=4)
    exchange(2, fv2, packed)

    def step2(x, h22):
        for k in range(BLOCKS):
            v, q = operate(x, k, 2, fv2)
            h22 = h22 + v * q
        return h22

    h22 = lax.fori_loop(0, NXL, step2, zero, unroll=4)

    sub = lax.broadcasted_iota(jnp.int32, (8, NZL), 0)
    level = [(value, None) for value in (g0, g2, h00, h01, h02, h11, h12, h22)]
    for width in (4, 2, 1):
        keep = lax.rem(sub // width, 2) == 0
        merged = []
        n = len(level) // 2
        for i in range(n):
            (ah, al), (bh, bl) = level[i], level[i + n]
            hi, err = two_sum(jnp.where(keep, ah, bh), roll_rows(jnp.where(keep, bh, ah), width, keep))
            if al is not None:
                err = err + (jnp.where(keep, al, bl) + roll_rows(jnp.where(keep, bl, al), width, keep))
            merged.append((hi, err))
        level = merged
    hi, lo = level[0]
    for width in (64, 32, 16, 8, 4, 2, 1):
        hi, err = two_sum(hi, roll(hi, width, 1))
        lo = (lo + roll(lo, width, 1)) + err
    own_row = jnp.where(lane == sub, hi, 0.0) + jnp.where(lane == sub + 64, lo, 0.0)
    row = jnp.sum(own_row, axis=0, keepdims=True)

    low_half = lax.broadcasted_iota(jnp.int32, (1, NZL), 1) < 64

    for phase, axis in enumerate(("gy", "gx", "gz")):
        slots = sums.at[phase]
        sums[phase, pos[axis]] = row
        copies = []
        for d in (4, 3, 5, 2, 6, 1, 7):
            copies.append(
                remote(
                    slots.at[pos[axis]], slots.at[pos[axis]],
                    sendr.at[phase, d - 1], recvr.at[phase, d - 1],
                    {axis: lax.rem(pos[axis] + d, RING)},
                )
            )
        for copy in copies:
            copy.start()
        if phase == 0:
            def terms(x, carry):
                for k in range(BLOCKS):
                    r = TOP + 8 * k
                    rows, own = pl.ds(r, 8), pl.ds(8 * k, 8)
                    p = fp[x + 1, rows]
                    pe = place(x, k, zmix[1])
                    gu = (
                        -0.5 * (fp[x + 2, rows] - p),
                        -0.5 * (fp[x + 1, pl.ds(r + 1, 8)] - p),
                        -0.5 * (above(p, pe) - p),
                    )
                    gd = (
                        -0.5 * (p - fp[x, rows]),
                        -0.5 * (p - fp[x + 1, pl.ds(r - 1, 8)]),
                        -0.5 * (p - below(p, pe)),
                    )
                    u2 = fu2[x + 1, rows]
                    bases[0, x, own] = (
                        (gd[0] * fu0[x, rows] + gu[0] * fu0[x + 1, rows])
                        + (gd[1] * fu1[x + 1, pl.ds(r - 1, 8)] + gu[1] * fu1[x + 1, rows])
                        + (gd[2] * below(u2, place(x, k, zmix[2])) + gu[2] * u2)
                    )
                    for i, field in enumerate((fv0, fv1, fv2)):
                        v, up, down = around(x, k, i, field)
                        total = None
                        for dim in range(3):
                            upper, lower = up[dim] - v, v - down[dim]
                            grads[i, dim, x, own] = upper
                            term = gd[dim] * lower + gu[dim] * upper
                            total = term if total is None else total + term
                        bases[1 + i, x, own] = total
                return carry

            lax.fori_loop(0, NXL, terms, 0)
        for copy in copies:
            copy.wait()
        parts = [sums[phase, i] for i in range(RING)]
        errs = []
        while len(parts) > 1:
            pairs = [two_sum(parts[i], parts[i + 1]) for i in range(0, len(parts), 2)]
            parts = [s for s, _ in pairs]
            errs.append(sum_tree([e for _, e in pairs]))
        total, err = parts[0], sum_tree(errs)
        row = jnp.where(low_half, total, total + roll(err, 64, 1))

    spread = jnp.broadcast_to(row, (8, NZL))
    col_hi = jnp.sum(jnp.where(lane == sub, spread, 0.0), axis=1, keepdims=True)
    col_lo = jnp.sum(jnp.where(lane == sub + 64, spread, 0.0), axis=1, keepdims=True)
    col_hi = jnp.broadcast_to(col_hi, (8, NZL))
    col_lo = jnp.broadcast_to(col_lo, (8, NZL))
    order = ROW_OF
    sums_hi_lo = [(col_hi[order[i] : order[i] + 1], col_lo[order[i] : order[i] + 1]) for i in range(8)]
    y = [jnp.broadcast_to(value, (8, NZL)) for value in galerkin(sums_hi_lo)]

    def finish(x, carry):
        for k in range(BLOCKS):
            rows, own = pl.ds(TOP + 8 * k, 8), pl.ds(8 * k, 8)
            for dim, field in enumerate((fu0, fu1, fu2)):
                grad = y[0] * grads[0, dim, x, own] + y[1] * grads[1, dim, x, own] + y[2] * grads[2, dim, x, own]
                out_u[dim, x, own] = field[x + 1, rows] + grad
            out_c[x, own] = bases[0, x, own] + (
                y[0] * bases[1, x, own] + y[1] * bases[2, x, own] + y[2] * bases[3, x, own]
            )
        return carry

    lax.fori_loop(0, NXL, finish, 0, unroll=4)
    stores = [
        pltpu.make_async_copy(out_u, ustar_hbm, store_sem.at[0]),
        pltpu.make_async_copy(out_c, coef_hbm, store_sem.at[1]),
    ]
    for store in stores:
        store.start()
    for copy in round1:
        copy.wait_send()
    for store in stores:
        store.wait()


def roll_rows(x, width, keep):
    if width == 4:
        return roll(x, 4, 0)
    return jnp.where(keep, roll(x, 8 - width, 0), roll(x, width, 0))


def sum_tree(values):
    total = values[0]
    for value in values[1:]:
        total = total + value
    return total


def row_order():
    level = [{i: set(range(8))} for i in range(8)]
    names = [[i] * 8 for i in range(8)]
    for width in (4, 2, 1):
        n = len(names) // 2
        names = [
            [names[i][r] if (r // width) % 2 == 0 else names[i + n][r] for r in range(8)] for i in range(n)
        ]
    return [names[0].index(i) for i in range(8)]


ROW_OF = row_order()


def on_device(phase_mask, pressure, velocity_cot):
    field = pltpu.VMEM((NXL + 2, 48, NZL), F32)
    block = pltpu.VMEM((NXL, NYL, NZL), F32)
    dma = pltpu.SemaphoreType.DMA
    anywhere = pl.BlockSpec(memory_space=pl.ANY)
    return pl.pallas_call(
        body,
        out_shape=(
            jax.ShapeDtypeStruct((3, NXL, NYL, NZL), F32),
            jax.ShapeDtypeStruct((NXL, NYL, NZL), F32),
        ),
        in_specs=[anywhere] * 3,
        out_specs=(anywhere, anywhere),
        scratch_shapes=[
            pltpu.VMEM((NXL, NYL, NZL), jnp.int32),
            field, field, field, field, field, field, field, field,
            pltpu.VMEM((NXL + 1, NYL, NZL), F32),
            block, block, block, block, block, block, block,
            pltpu.VMEM((3, 3, NXL, NYL, NZL), F32),
            pltpu.VMEM((4, NXL, NYL, NZL), F32),
            pltpu.VMEM((3, NXL, NZL), F32),
            pltpu.VMEM((2, NXL, NZL), F32),
            pltpu.VMEM((3, NXL, NZL), F32),
            pltpu.VMEM((2, NXL, NZL), F32),
            pltpu.VMEM((NXL, NZL), F32),
            pltpu.VMEM((NXL, NZL), F32),
            pltpu.VMEM((3, NXL, NZL), F32),
            pltpu.VMEM((3, NXL, NZL), F32),
            pltpu.VMEM((3, 8, NZL), F32),
            pltpu.VMEM((3, 8, NZL), F32),
            pltpu.VMEM((3, 8, NZL), F32),
            pltpu.VMEM((3, 8, NZL), F32),
            pltpu.VMEM((3, 8, NZL), F32),
            pltpu.VMEM((3, 8, NZL), F32),
            pltpu.VMEM((3, 8, NZL), F32),
            pltpu.VMEM((3, 8, NZL), F32),
            pltpu.VMEM((3, RING, 1, NZL), F32),
            pltpu.VMEM((3, NXL, NYL, NZL), F32),
            block,
            dma((5,)), dma((2,)),
            dma((9,)), dma((9,)), dma((3, 6)), dma((3, 6)), dma((3, 7)), dma((3, 7)),
        ],
        compiler_params=pltpu.CompilerParams(collective_id=0, has_side_effects=True),
        name="projection_adjoint",
    )(phase_mask, pressure, velocity_cot)


def solution(mesh):
    in_specs = (P("gx", "gy", "gz"), P("gx", "gy", "gz"), P(None, "gx", "gy", "gz"))
    out_specs = (P(None, "gx", "gy", "gz"), P("gx", "gy", "gz"))
    return jax.shard_map(
        on_device, mesh=mesh, in_specs=in_specs, out_specs=out_specs, check_vma=False
    )
```

```python
import jax
import jax.numpy as jnp
from jax import lax
from jax.experimental import pallas as pl
from jax.experimental.pallas import tpu as pltpu
from jax.sharding import PartitionSpec as P


MESH = pl.DeviceIdType.MESH
AXES = ("gx", "gy", "gz")
RING = 8
NXL, NYL, NZL = 16, 32, 128
TOP = 8
LAST = TOP + NYL - 1
BLOCKS = NYL // 8
F32 = jnp.float32
PHASES = (("gy",), ("gx", "gz"))


def two_sum(a, b):
    s = a + b
    t = s - a
    return s, (a - (s - t)) + (b - t)


def split(a):
    c = 4097.0 * a
    hi = c - (c - a)
    return hi, a - hi


def sub_mul(x, c, y):
    p = c * y[0]
    ch, cl = split(c)
    yh, yl = split(y[0])
    err = ((ch * yh - p) + ch * yl + cl * yh) + cl * yl
    s, t = two_sum(x[0], -p)
    t = t + (x[1] - (err + c * y[1]))
    hi = s + t
    return hi, t - (hi - s)


def galerkin(sums):
    g0, g2, h00, h01, h02, h11, h12, h22 = sums
    one = jnp.ones_like(g0[0])
    g1 = sub_mul(h00, one, g0)
    a = h01[0] / h00[0]
    b = h02[0] / h00[0]
    h01p = sub_mul(h01, a, h00)
    h02p = sub_mul(h02, b, h00)
    h11p = sub_mul(sub_mul(h11, a, h01), a, h01p)
    h12p = sub_mul(sub_mul(h12, a, h02), b, h01p)
    h22p = sub_mul(sub_mul(h22, b, h02), b, h02p)
    g1p = sub_mul(g1, a, g0)
    g2p = sub_mul(g2, b, g0)
    ok1 = h11p[0] > 1e-10 * h11[0]
    inv1 = jnp.where(ok1, 1.0 / jnp.where(ok1, h11p[0], 1.0), 0.0)
    c = h12p[0] * inv1
    h12q = sub_mul(h12p, c, h11p)
    h22q = sub_mul(sub_mul(h22p, c, h12p), c, h12q)
    g2q = sub_mul(g2p, c, g1p)
    h02q = h02p[0] - c * h01p[0]
    ok2 = h22q[0] > 1e-10 * h22[0]
    y2 = jnp.where(ok2, g2q[0] / jnp.where(ok2, h22q[0], 1.0), 0.0)
    y1p = (g1p[0] - h12q[0] * y2) * inv1
    y0p = (g0[0] - h01p[0] * y1p - h02q * y2) / h00[0]
    return y0p - a * y1p - (b - c * a) * y2, y1p - c * y2, y2


def roll(x, shift, axis):
    return pltpu.roll(x, shift, axis)


def remote(src, dst, send, recv, device):
    return pltpu.make_async_remote_copy(
        src_ref=src, dst_ref=dst, send_sem=send, recv_sem=recv, device_id=device, device_id_type=MESH
    )


def body(
    mask_hbm, press_hbm, vel_hbm, out_u, out_c,
    mask, fc, fp, fu0, fu1, fu2, fv0, fv1, fv2,
    wx, wyu, wyd, wzu, wzd, minv, rhs, img,
    grads, bases,
    yup, ydn, yup_in, ydn_in, pyup, pydn, pyup_in, pydn_in, vyup, vydn, vyup_in, vydn_in,
    zup, zin_lo, zin_hi, pz, pz_lo, pz_hi, zmix, vz, vz_lo, vz_hi, vmix,
    sums,
    load_sem,
    send1, recv1, sendv, recvv, sendr, recvr, ready,
):
    pos = {axis: lax.axis_index(axis) for axis in AXES}
    fwd = {axis: lax.rem(pos[axis] + 1, RING) for axis in AXES}
    bwd = {axis: lax.rem(pos[axis] + RING - 1, RING) for axis in AXES}
    lane = lax.broadcasted_iota(jnp.int32, (8, NZL), 1)
    half = lane // 2
    even = lane - 2 * half == 0
    first = lane == 0
    final = lane == NZL - 1

    cells = (pl.ds(1, NXL), pl.ds(TOP, NYL))
    loads = [pltpu.make_async_copy(mask_hbm, mask, load_sem.at[0])]
    for i, field in enumerate((fu0, fu1, fu2)):
        loads.append(pltpu.make_async_copy(vel_hbm.at[i], field.at[cells], load_sem.at[1 + i]))
    loads.append(pltpu.make_async_copy(press_hbm, fp.at[cells], load_sem.at[4]))
    for load in loads:
        load.start()

    barrier = pltpu.get_barrier_semaphore()
    for axis in AXES:
        for other in (fwd[axis], bwd[axis]):
            pl.semaphore_signal(barrier, inc=1, device_id={axis: other}, device_id_type=MESH)
    for load in loads:
        load.wait()

    def pick(x, k, value, packed):
        return jnp.where(half == BLOCKS * x + k, roll(value, 2 * BLOCKS * x + 2 * k + 1, 1), packed)

    def place(x, k, mixed):
        return roll(mixed, NZL - 1 - 2 * BLOCKS * x - 2 * k, 1)

    def above(value, edge):
        return jnp.where(final, edge, roll(value, NZL - 1, 1))

    def below(value, edge):
        return jnp.where(first, edge, roll(value, 1, 1))

    zero = jnp.zeros((8, NZL), F32)

    def prepare(x, carry):
        pc, pp, pu = carry
        for k in range(BLOCKS):
            rows = pl.ds(TOP + 8 * k, 8)
            phase = mask[x, pl.ds(8 * k, 8)]
            c = jnp.where(phase == 0, 8.0, jnp.where(phase == 1, 1.0, 2.0)).astype(F32)
            fc[x + 1, rows] = c
            pc = pick(x, k, c, pc)
            pp = pick(x, k, fp[x + 1, rows], pp)
            pu = pick(x, k, fu2[x + 1, rows], pu)
            if k == 0:
                ydn[pl.ds(x, 1)] = c[0:1]
                pydn[pl.ds(x, 1)] = fp[x + 1, pl.ds(TOP, 1)]
            if k == BLOCKS - 1:
                yup[0, pl.ds(x, 1)] = c[7:8]
                pyup[pl.ds(x, 1)] = fp[x + 1, pl.ds(LAST, 1)]
                yup[1, pl.ds(x, 1)] = fu1[x + 1, pl.ds(LAST, 1)]
        return pc, pp, pu

    pc, pp, pu = lax.fori_loop(0, NXL, prepare, (zero, zero, zero), unroll=4)
    zup[0] = pc
    zup[1] = pu
    pz[...] = pp

    pl.semaphore_wait(barrier, 6)

    inner = pl.ds(TOP, NYL)
    round1 = [
        remote(fc.at[NXL, inner], fc.at[0, inner], send1.at[0], recv1.at[0], {"gx": fwd["gx"]}),
        remote(fc.at[1, inner], fc.at[NXL + 1, inner], send1.at[1], recv1.at[1], {"gx": bwd["gx"]}),
        remote(yup, yup_in, send1.at[2], recv1.at[2], {"gy": fwd["gy"]}),
        remote(ydn, ydn_in, send1.at[3], recv1.at[3], {"gy": bwd["gy"]}),
        remote(zup, zin_lo, send1.at[4], recv1.at[4], {"gz": fwd["gz"]}),
        remote(zup, zin_hi, send1.at[5], recv1.at[5], {"gz": bwd["gz"]}),
        remote(fu0.at[NXL, inner], fu0.at[0, inner], send1.at[6], recv1.at[6], {"gx": fwd["gx"]}),
    ]
    for copy in round1:
        copy.start()
    later = [
        remote(fp.at[NXL, inner], fp.at[0, inner], send1.at[7], recv1.at[7], {"gx": fwd["gx"]}),
        remote(fp.at[1, inner], fp.at[NXL + 1, inner], send1.at[8], recv1.at[8], {"gx": bwd["gx"]}),
        remote(pyup, pyup_in, send1.at[9], recv1.at[9], {"gy": fwd["gy"]}),
        remote(pydn, pydn_in, send1.at[10], recv1.at[10], {"gy": bwd["gy"]}),
        remote(pz, pz_lo, send1.at[11], recv1.at[11], {"gz": fwd["gz"]}),
        remote(pz, pz_hi, send1.at[12], recv1.at[12], {"gz": bwd["gz"]}),
    ]
    for copy in round1:
        copy.wait_recv()
    sent = round1 + later

    low = {axis: pos[axis] == 0 for axis in AXES}
    high = {axis: pos[axis] == RING - 1 for axis in AXES}

    def clear_x(fields_low, fields_high):
        @pl.when(low["gx"])
        def _():
            for field in fields_low:
                field[0, inner] = jnp.zeros((NYL, NZL), F32)

        @pl.when(high["gx"])
        def _():
            for field in fields_high:
                field[NXL + 1, inner] = jnp.zeros((NYL, NZL), F32)

    def mix(lo, hi):
        lo = jnp.where(low["gz"], 0.0, lo)
        hi = jnp.where(high["gz"], 0.0, hi)
        return jnp.where(even, roll(hi, NZL - 1, 1), roll(lo, 1, 1))

    clear_x((fc, fu0), (fc,))
    zmix[0] = mix(zin_lo[0], zin_hi[0])
    zmix[2] = mix(zin_lo[1], zin_hi[1])
    for x in range(NXL):
        row = pl.ds(x, 1)
        fc[x + 1, pl.ds(TOP - 1, 1)] = jnp.where(low["gy"], 0.0, yup_in[0, row])
        fu1[x + 1, pl.ds(TOP - 1, 1)] = jnp.where(low["gy"], 0.0, yup_in[1, row])
        fc[x + 1, pl.ds(LAST + 1, 1)] = jnp.where(high["gy"], 0.0, ydn_in[row])

    wx[0] = 0.5 * (fc[0, inner] + fc[1, inner])

    def faces(i, x, k, value):
        if k == 0:
            vydn[i, pl.ds(x, 1)] = value[0:1]
        if k == BLOCKS - 1:
            vyup[i, pl.ds(x, 1)] = value[7:8]

    def start(x, carry):
        packed, g0 = carry
        for k in range(BLOCKS):
            r = TOP + 8 * k
            rows, own = pl.ds(r, 8), pl.ds(8 * k, 8)
            c = fc[x + 1, rows]
            edge = place(x, k, zmix[0])
            xu = 0.5 * (c + fc[x + 2, rows])
            xd = wx[x, own]
            yu = 0.5 * (c + fc[x + 1, pl.ds(r + 1, 8)])
            yd = 0.5 * (c + fc[x + 1, pl.ds(r - 1, 8)])
            zu = 0.5 * (c + above(c, edge))
            zd = 0.5 * (c + below(c, edge))
            m = 1.0 / ((xd + xu) + (yd + yu) + (zd + zu))
            u2 = fu2[x + 1, rows]
            r0 = (
                (xu * fu0[x + 1, rows] - xd * fu0[x, rows])
                + (yu * fu1[x + 1, rows] - yd * fu1[x + 1, pl.ds(r - 1, 8)])
                + (zu * u2 - zd * below(u2, place(x, k, zmix[2])))
            )
            v = m * r0
            wx[x + 1, own] = xu
            wyu[x, own] = yu
            wyd[x, own] = yd
            wzu[x, own] = zu
            wzd[x, own] = zd
            minv[x, own] = m
            rhs[x, own] = r0
            fv0[x + 1, rows] = v
            packed = pick(x, k, v, packed)
            faces(0, x, k, v)
            g0 = g0 + v * r0
        return packed, g0

    packed, g0 = lax.fori_loop(0, NXL, start, (zero, zero), unroll=4)

    def exchange(i, field, packed):
        vz[i] = packed
        copies = [
            remote(field.at[NXL, inner], field.at[0, inner], sendv.at[i, 0], recvv.at[i, 0], {"gx": fwd["gx"]}),
            remote(field.at[1, inner], field.at[NXL + 1, inner], sendv.at[i, 1], recvv.at[i, 1], {"gx": bwd["gx"]}),
            remote(vyup.at[i], vyup_in.at[i], sendv.at[i, 2], recvv.at[i, 2], {"gy": fwd["gy"]}),
            remote(vydn.at[i], vydn_in.at[i], sendv.at[i, 3], recvv.at[i, 3], {"gy": bwd["gy"]}),
            remote(vz.at[i], vz_lo.at[i], sendv.at[i, 4], recvv.at[i, 4], {"gz": fwd["gz"]}),
            remote(vz.at[i], vz_hi.at[i], sendv.at[i, 5], recvv.at[i, 5], {"gz": bwd["gz"]}),
        ]
        for copy in copies:
            copy.start()
        if i == 0:
            for copy in later:
                copy.start()
        for copy in copies:
            copy.wait_recv()
        sent.extend(copies)
        clear_x((field,), (field,))
        vmix[i] = mix(vz_lo[i], vz_hi[i])
        for x in range(NXL):
            row = pl.ds(x, 1)
            field[x + 1, pl.ds(TOP - 1, 1)] = jnp.where(low["gy"], 0.0, vyup_in[i, row])
            field[x + 1, pl.ds(LAST + 1, 1)] = jnp.where(high["gy"], 0.0, vydn_in[i, row])

    def around(x, k, i, field):
        r = TOP + 8 * k
        rows = pl.ds(r, 8)
        v = field[x + 1, rows]
        edge = place(x, k, vmix[i])
        return (
            v,
            (field[x + 2, rows], field[x + 1, pl.ds(r + 1, 8)], above(v, edge)),
            (field[x, rows], field[x + 1, pl.ds(r - 1, 8)], below(v, edge)),
        )

    def operate(x, k, i, field):
        own = pl.ds(8 * k, 8)
        v, (xp, yp, zp), (xm, ym, zm) = around(x, k, i, field)
        image = (
            (wx[x, own] * (v - xm) + wx[x + 1, own] * (v - xp))
            + (wyd[x, own] * (v - ym) + wyu[x, own] * (v - yp))
            + (wzd[x, own] * (v - zm) + wzu[x, own] * (v - zp))
        )
        return v, image

    exchange(0, fv0, packed)

    def step0(x, carry):
        packed, h00, h01 = carry
        for k in range(BLOCKS):
            own = pl.ds(8 * k, 8)
            v, q = operate(x, k, 0, fv0)
            w = minv[x, own] * q - v
            img[x, own] = q
            fv1[x + 1, pl.ds(TOP + 8 * k, 8)] = w
            packed = pick(x, k, w, packed)
            faces(1, x, k, w)
            h00 = h00 + v * q
            h01 = h01 + w * q
        return packed, h00, h01

    packed, h00, h01 = lax.fori_loop(0, NXL, step0, (zero, zero, zero), unroll=4)
    exchange(1, fv1, packed)
    for d in range(1, RING):
        pl.semaphore_signal(
            ready, inc=1, device_id={"gz": lax.rem(pos["gz"] + d, RING)}, device_id_type=MESH
        )

    def step1(x, carry):
        packed, h02, h11, h12, g2 = carry
        for k in range(BLOCKS):
            own = pl.ds(8 * k, 8)
            v, q = operate(x, k, 1, fv1)
            w = minv[x, own] * q - v
            fv2[x + 1, pl.ds(TOP + 8 * k, 8)] = w
            packed = pick(x, k, w, packed)
            faces(2, x, k, w)
            h02 = h02 + w * img[x, own]
            h11 = h11 + v * q
            h12 = h12 + w * q
            g2 = g2 + w * rhs[x, own]
        return packed, h02, h11, h12, g2

    packed, h02, h11, h12, g2 = lax.fori_loop(0, NXL, step1, (zero,) * 5, unroll=4)
    exchange(2, fv2, packed)

    def step2(x, h22):
        for k in range(BLOCKS):
            v, q = operate(x, k, 2, fv2)
            h22 = h22 + v * q
        return h22

    h22 = lax.fori_loop(0, NXL, step2, zero, unroll=4)

    sub = lax.broadcasted_iota(jnp.int32, (8, NZL), 0)
    level = [(value, None) for value in (g0, g2, h00, h01, h02, h11, h12, h22)]
    for width in (4, 2, 1):
        keep = lax.rem(sub // width, 2) == 0
        merged = []
        n = len(level) // 2
        for i in range(n):
            (ah, al), (bh, bl) = level[i], level[i + n]
            hi, err = two_sum(jnp.where(keep, ah, bh), roll_rows(jnp.where(keep, bh, ah), width, keep))
            if al is not None:
                err = err + (jnp.where(keep, al, bl) + roll_rows(jnp.where(keep, bl, al), width, keep))
            merged.append((hi, err))
        level = merged
    hi, lo = level[0]
    for width in (64, 32, 16, 8, 4, 2, 1):
        hi, err = two_sum(hi, roll(hi, width, 1))
        lo = (lo + roll(lo, width, 1)) + err
    own_row = jnp.where(lane == sub, hi, 0.0) + jnp.where(lane == sub + 64, lo, 0.0)
    row = jnp.sum(own_row, axis=0, keepdims=True)

    low_half = lax.broadcasted_iota(jnp.int32, (1, NZL), 1) < 64

    slot0 = 0
    drains = []
    for phase, axes in enumerate(PHASES):
        count = RING ** len(axes)
        mine = 0
        for axis in axes:
            mine = mine * RING + pos[axis]
        slots = sums.at[pl.ds(slot0, count)]
        slots[mine] = row
        if len(axes) > 1:
            pl.semaphore_wait(ready, RING - 1)
        offsets = [()]
        for axis in axes:
            offsets = [o + (d,) for o in offsets for d in range(RING)]
        offsets = sorted(offsets[1:], key=lambda o: -sum(min(d, RING - d) for d in o))
        for o in offsets:
            device = {axis: lax.rem(pos[axis] + d, RING) for axis, d in zip(axes, o) if d}
            remote(slots.at[mine], slots.at[mine], sendr.at[phase], recvr.at[phase], device).start()
        if phase == 0:
            for copy in later:
                copy.wait_recv()
            clear_x((fp,), (fp,))
            zmix[1] = mix(pz_lo[...], pz_hi[...])
            for x in range(NXL):
                lrow = pl.ds(x, 1)
                fp[x + 1, pl.ds(TOP - 1, 1)] = jnp.where(low["gy"], 0.0, pyup_in[lrow])
                fp[x + 1, pl.ds(LAST + 1, 1)] = jnp.where(high["gy"], 0.0, pydn_in[lrow])

            def terms(x, carry):
                for k in range(BLOCKS):
                    r = TOP + 8 * k
                    rows, own = pl.ds(r, 8), pl.ds(8 * k, 8)
                    p = fp[x + 1, rows]
                    pe = place(x, k, zmix[1])
                    gu = (
                        -0.5 * (fp[x + 2, rows] - p),
                        -0.5 * (fp[x + 1, pl.ds(r + 1, 8)] - p),
                        -0.5 * (above(p, pe) - p),
                    )
                    gd = (
                        -0.5 * (p - fp[x, rows]),
                        -0.5 * (p - fp[x + 1, pl.ds(r - 1, 8)]),
                        -0.5 * (p - below(p, pe)),
                    )
                    u2 = fu2[x + 1, rows]
                    bases[0, x, own] = (
                        (gd[0] * fu0[x, rows] + gu[0] * fu0[x + 1, rows])
                        + (gd[1] * fu1[x + 1, pl.ds(r - 1, 8)] + gu[1] * fu1[x + 1, rows])
                        + (gd[2] * below(u2, place(x, k, zmix[2])) + gu[2] * u2)
                    )
                    for i, field in enumerate((fv0, fv1, fv2)):
                        v, up, down = around(x, k, i, field)
                        total = None
                        for dim in range(3):
                            upper, lower = up[dim] - v, v - down[dim]
                            grads[i, dim, x, own] = upper
                            term = gd[dim] * lower + gu[dim] * upper
                            total = term if total is None else total + term
                        bases[1 + i, x, own] = total
                return carry

            lax.fori_loop(0, NXL, terms, 0)
        others = sums.at[pl.ds(slot0, count - 1)]
        pltpu.make_async_copy(others, others, recvr.at[phase]).wait()
        drains.append(pltpu.make_async_copy(others, others, sendr.at[phase]))
        parts = [sums[slot0 + i] for i in range(count)]
        errs = []
        while len(parts) > 1:
            pairs = [two_sum(parts[i], parts[i + 1]) for i in range(0, len(parts), 2)]
            parts = [s for s, _ in pairs]
            errs.append(sum_tree([e for _, e in pairs]))
        total, err = parts[0], sum_tree(errs)
        row = jnp.where(low_half, total, total + roll(err, 64, 1))
        slot0 += count

    spread = jnp.broadcast_to(row, (8, NZL))
    col_hi = jnp.sum(jnp.where(lane == sub, spread, 0.0), axis=1, keepdims=True)
    col_lo = jnp.sum(jnp.where(lane == sub + 64, spread, 0.0), axis=1, keepdims=True)
    col_hi = jnp.broadcast_to(col_hi, (8, NZL))
    col_lo = jnp.broadcast_to(col_lo, (8, NZL))
    order = ROW_OF
    sums_hi_lo = [(col_hi[order[i] : order[i] + 1], col_lo[order[i] : order[i] + 1]) for i in range(8)]
    y = [jnp.broadcast_to(value, (8, NZL)) for value in galerkin(sums_hi_lo)]

    def finish(x, carry):
        for k in range(BLOCKS):
            rows, own = pl.ds(TOP + 8 * k, 8), pl.ds(8 * k, 8)
            for dim, field in enumerate((fu0, fu1, fu2)):
                grad = y[0] * grads[0, dim, x, own] + y[1] * grads[1, dim, x, own] + y[2] * grads[2, dim, x, own]
                out_u[dim, x, own] = field[x + 1, rows] + grad
            out_c[x, own] = bases[0, x, own] + (
                y[0] * bases[1, x, own] + y[1] * bases[2, x, own] + y[2] * bases[3, x, own]
            )
        return carry

    lax.fori_loop(0, NXL, finish, 0, unroll=4)
    for drain in drains:
        drain.wait()
    for copy in sent:
        copy.wait_send()


def roll_rows(x, width, keep):
    if width == 4:
        return roll(x, 4, 0)
    return jnp.where(keep, roll(x, 8 - width, 0), roll(x, width, 0))


def sum_tree(values):
    total = values[0]
    for value in values[1:]:
        total = total + value
    return total


def row_order():
    level = [{i: set(range(8))} for i in range(8)]
    names = [[i] * 8 for i in range(8)]
    for width in (4, 2, 1):
        n = len(names) // 2
        names = [
            [names[i][r] if (r // width) % 2 == 0 else names[i + n][r] for r in range(8)] for i in range(n)
        ]
    return [names[0].index(i) for i in range(8)]


ROW_OF = row_order()


def save(ustar, coef, ustar_hbm, coef_hbm, sem):
    stores = [
        pltpu.make_async_copy(ustar, ustar_hbm, sem.at[0]),
        pltpu.make_async_copy(coef, coef_hbm, sem.at[1]),
    ]
    for store in stores:
        store.start()
    for store in stores:
        store.wait()


def on_device(phase_mask, pressure, velocity_cot):
    field = pltpu.VMEM((NXL + 2, 48, NZL), F32)
    block = pltpu.VMEM((NXL, NYL, NZL), F32)
    flat = pltpu.VMEM((NXL, NZL), F32)
    flats = pltpu.VMEM((3, NXL, NZL), F32)
    tile = pltpu.VMEM((8, NZL), F32)
    tiles = pltpu.VMEM((3, 8, NZL), F32)
    dma = pltpu.SemaphoreType.DMA
    in_hbm = pl.BlockSpec(memory_space=pltpu.HBM)
    in_vmem = pl.BlockSpec(memory_space=pltpu.VMEM)
    out_shape = (
        jax.ShapeDtypeStruct((3, NXL, NYL, NZL), F32),
        jax.ShapeDtypeStruct((NXL, NYL, NZL), F32),
    )
    inputs = [
        pltpu.with_memory_space_constraint(a, pltpu.HBM) for a in (phase_mask, pressure, velocity_cot)
    ]
    outs = pl.pallas_call(
        body,
        out_shape=out_shape,
        in_specs=[in_hbm] * 3,
        out_specs=(in_vmem, in_vmem),
        scratch_shapes=[
            pltpu.VMEM((NXL, NYL, NZL), jnp.int32),
            *[field] * 8,
            pltpu.VMEM((NXL + 1, NYL, NZL), F32),
            *[block] * 7,
            pltpu.VMEM((3, 3, NXL, NYL, NZL), F32),
            pltpu.VMEM((4, NXL, NYL, NZL), F32),
            pltpu.VMEM((2, NXL, NZL), F32), flat, pltpu.VMEM((2, NXL, NZL), F32), flat,
            *[flat] * 4,
            *[flats] * 4,
            *[pltpu.VMEM((2, 8, NZL), F32)] * 3,
            *[tile] * 3,
            *[tiles] * 5,
            pltpu.VMEM((sum(RING ** len(axes) for axes in PHASES), 1, NZL), F32),
            dma((5,)),
            dma((13,)), dma((13,)), dma((3, 6)), dma((3, 6)),
            dma((len(PHASES),)), dma((len(PHASES),)),
            pltpu.SemaphoreType.REGULAR,
        ],
        compiler_params=pltpu.CompilerParams(
            collective_id=0, has_side_effects=True, vmem_limit_bytes=24 * 1024 * 1024
        ),
        name="projection_adjoint",
    )(*inputs)
    return pl.pallas_call(
        save,
        out_shape=out_shape,
        in_specs=[in_vmem] * 2,
        out_specs=(in_hbm, in_hbm),
        scratch_shapes=[dma((2,))],
        compiler_params=pltpu.CompilerParams(vmem_limit_bytes=4 * 1024 * 1024),
        name="save",
    )(*outs)


def solution(mesh):
    in_specs = (P("gx", "gy", "gz"), P("gx", "gy", "gz"), P(None, "gx", "gy", "gz"))
    out_specs = (P(None, "gx", "gy", "gz"), P("gx", "gy", "gz"))
    return jax.shard_map(
        on_device, mesh=mesh, in_specs=in_specs, out_specs=out_specs, check_vma=False
    )
```

```python
import jax
import jax.numpy as jnp
from jax import lax
from jax.experimental import pallas as pl
from jax.experimental.pallas import tpu as pltpu
from jax.sharding import PartitionSpec as P


MESH = pl.DeviceIdType.MESH
AXES = ("gx", "gy", "gz")
RING = 8
NXL, NYL, NZL = 16, 32, 128
TOP = 8
LAST = TOP + NYL - 1
BLOCKS = NYL // 8
F32 = jnp.float32
PHASES = (("gy",), ("gx", "gz"))


def two_sum(a, b):
    s = a + b
    t = s - a
    return s, (a - (s - t)) + (b - t)


def split(a):
    c = 4097.0 * a
    hi = c - (c - a)
    return hi, a - hi


def sub_mul(x, c, y):
    p = c * y[0]
    ch, cl = split(c)
    yh, yl = split(y[0])
    err = ((ch * yh - p) + ch * yl + cl * yh) + cl * yl
    s, t = two_sum(x[0], -p)
    t = t + (x[1] - (err + c * y[1]))
    hi = s + t
    return hi, t - (hi - s)


def galerkin(sums):
    g0, g2, h00, h01, h02, h11, h12, h22 = sums
    one = jnp.ones_like(g0[0])
    g1 = sub_mul(h00, one, g0)
    a = h01[0] / h00[0]
    b = h02[0] / h00[0]
    h01p = sub_mul(h01, a, h00)
    h02p = sub_mul(h02, b, h00)
    h11p = sub_mul(sub_mul(h11, a, h01), a, h01p)
    h12p = sub_mul(sub_mul(h12, a, h02), b, h01p)
    h22p = sub_mul(sub_mul(h22, b, h02), b, h02p)
    g1p = sub_mul(g1, a, g0)
    g2p = sub_mul(g2, b, g0)
    ok1 = h11p[0] > 1e-10 * h11[0]
    inv1 = jnp.where(ok1, 1.0 / jnp.where(ok1, h11p[0], 1.0), 0.0)
    c = h12p[0] * inv1
    h12q = sub_mul(h12p, c, h11p)
    h22q = sub_mul(sub_mul(h22p, c, h12p), c, h12q)
    g2q = sub_mul(g2p, c, g1p)
    h02q = h02p[0] - c * h01p[0]
    ok2 = h22q[0] > 1e-10 * h22[0]
    y2 = jnp.where(ok2, g2q[0] / jnp.where(ok2, h22q[0], 1.0), 0.0)
    y1p = (g1p[0] - h12q[0] * y2) * inv1
    y0p = (g0[0] - h01p[0] * y1p - h02q * y2) / h00[0]
    return y0p - a * y1p - (b - c * a) * y2, y1p - c * y2, y2


def roll(x, shift, axis):
    return pltpu.roll(x, shift, axis)


def remote(src, dst, send, recv, device):
    return pltpu.make_async_remote_copy(
        src_ref=src, dst_ref=dst, send_sem=send, recv_sem=recv, device_id=device, device_id_type=MESH
    )


def body(
    mask_hbm, press_hbm, vel_hbm, out_u, out_c,
    mask, fc, fp, fu0, fu1, fu2, fv0, fv1, fv2,
    wx, wyu, wyd, wzu, wzd, wzb, wyb, minv, rhs, img, part,
    grads, bases,
    yup, ydn, yup_in, ydn_in, pyup, pydn, pyup_in, pydn_in, vyup, vydn, vy_in, vx_in,
    zup, zin_lo, zin_hi, pz, pz_lo, pz_hi, zmix, vz, vz_lo, vz_hi, vmix,
    sums,
    load_sem,
    send1, recv1, sendv, recvv, sendr, recvr, ready, token,
):
    pos = {axis: lax.axis_index(axis) for axis in AXES}
    fwd = {axis: lax.rem(pos[axis] + 1, RING) for axis in AXES}
    bwd = {axis: lax.rem(pos[axis] + RING - 1, RING) for axis in AXES}
    lane = lax.broadcasted_iota(jnp.int32, (8, NZL), 1)
    half = lane // 2
    even = lane - 2 * half == 0
    first = lane == 0
    final = lane == NZL - 1

    low = {axis: pos[axis] == 0 for axis in AXES}
    high = {axis: pos[axis] == RING - 1 for axis in AXES}

    class Shift:
        def __init__(self, src, dst, send, recv, axis, up):
            other = fwd[axis] if up else bwd[axis]
            self.copy = remote(src, dst, send, recv, {axis: other})
            self.sends = jnp.logical_not(high[axis] if up else low[axis])
            self.receives = jnp.logical_not(low[axis] if up else high[axis])

        def start(self):
            pl.when(self.sends)(lambda: self.copy.start())

        def wait_recv(self):
            pl.when(self.receives)(lambda: self.copy.wait_recv())

        def wait_send(self):
            pl.when(self.sends)(lambda: self.copy.wait_send())

    def tell(stage):
        for a, axis in enumerate(AXES):
            for end, other in ((high[axis], fwd[axis]), (low[axis], bwd[axis])):

                @pl.when(end)
                def _(a=a, axis=axis, other=other):
                    pl.semaphore_signal(
                        token.at[stage, a], inc=1, device_id={axis: other}, device_id_type=MESH
                    )

    def heard(stage):
        for a, axis in enumerate(AXES):

            @pl.when(jnp.logical_or(high[axis], low[axis]))
            def _(a=a):
                pl.semaphore_wait(token.at[stage, a], 1)

    cells = (pl.ds(1, NXL), pl.ds(TOP, NYL))
    loads = [pltpu.make_async_copy(mask_hbm, mask, load_sem.at[0])]
    for i, field in enumerate((fu0, fu1, fu2)):
        loads.append(pltpu.make_async_copy(vel_hbm.at[i], field.at[cells], load_sem.at[1 + i]))
    loads.append(pltpu.make_async_copy(press_hbm, fp.at[cells], load_sem.at[4]))
    for load in loads:
        load.start()

    inner = pl.ds(TOP, NYL)
    plane = jnp.zeros((NYL, NZL), F32)
    line = jnp.zeros((1, NZL), F32)
    zero = jnp.zeros((8, NZL), F32)
    for field in (fc, fp, fu0, fv0, fv1, fv2):
        field[0, inner] = plane
        field[NXL + 1, inner] = plane
    for x in range(1, NXL + 1):
        for field in (fv0, fv1, fv2):
            field[x, pl.ds(TOP - 1, 1)] = line
            field[x, pl.ds(LAST + 1, 1)] = line
    for buffer in (yup_in, ydn_in, pyup_in, pydn_in, vy_in, vx_in, zin_lo, zin_hi, pz_lo, pz_hi, vz_lo, vz_hi):
        buffer[...] = jnp.zeros(buffer.shape, F32)

    barrier = pltpu.get_barrier_semaphore()
    for axis in AXES:
        for other in (fwd[axis], bwd[axis]):
            pl.semaphore_signal(barrier, inc=1, device_id={axis: other}, device_id_type=MESH)
    for load in loads:
        load.wait()

    def pick(x, k, value, packed):
        return jnp.where(half == BLOCKS * x + k, roll(value, 2 * BLOCKS * x + 2 * k + 1, 1), packed)

    def place(x, k, mixed):
        return roll(mixed, NZL - 1 - 2 * BLOCKS * x - 2 * k, 1)

    def above(value, edge):
        return jnp.where(final, edge, roll(value, NZL - 1, 1))

    def below(value, edge):
        return jnp.where(first, edge, roll(value, 1, 1))

    def prepare(x, carry):
        pc, pp, pu = carry
        for k in range(BLOCKS):
            rows = pl.ds(TOP + 8 * k, 8)
            phase = mask[x, pl.ds(8 * k, 8)]
            c = jnp.where(phase == 0, 8.0, jnp.where(phase == 1, 1.0, 2.0)).astype(F32)
            fc[x + 1, rows] = c
            pc = pick(x, k, c, pc)
            pp = pick(x, k, fp[x + 1, rows], pp)
            pu = pick(x, k, fu2[x + 1, rows], pu)
            if k == 0:
                ydn[pl.ds(x, 1)] = c[0:1]
                pydn[pl.ds(x, 1)] = fp[x + 1, pl.ds(TOP, 1)]
            if k == BLOCKS - 1:
                yup[0, pl.ds(x, 1)] = c[7:8]
                pyup[pl.ds(x, 1)] = fp[x + 1, pl.ds(LAST, 1)]
                yup[1, pl.ds(x, 1)] = fu1[x + 1, pl.ds(LAST, 1)]
        return pc, pp, pu

    pc, pp, pu = lax.fori_loop(0, NXL, prepare, (zero, zero, zero), unroll=4)
    zup[0] = pc
    zup[1] = pu
    pz[...] = pp

    pl.semaphore_wait(barrier, 6)

    round1 = [
        Shift(fc.at[NXL, inner], fc.at[0, inner], send1.at[0], recv1.at[0], "gx", True),
        Shift(fc.at[1, inner], fc.at[NXL + 1, inner], send1.at[1], recv1.at[1], "gx", False),
        Shift(yup, yup_in, send1.at[2], recv1.at[2], "gy", True),
        Shift(ydn, ydn_in, send1.at[3], recv1.at[3], "gy", False),
        Shift(zup, zin_lo, send1.at[4], recv1.at[4], "gz", True),
        Shift(zup, zin_hi, send1.at[5], recv1.at[5], "gz", False),
        Shift(fu0.at[NXL, inner], fu0.at[0, inner], send1.at[6], recv1.at[6], "gx", True),
    ]
    for copy in round1:
        copy.start()
    tell(0)
    later = [
        Shift(fp.at[NXL, inner], fp.at[0, inner], send1.at[7], recv1.at[7], "gx", True),
        Shift(fp.at[1, inner], fp.at[NXL + 1, inner], send1.at[8], recv1.at[8], "gx", False),
        Shift(pyup, pyup_in, send1.at[9], recv1.at[9], "gy", True),
        Shift(pydn, pydn_in, send1.at[10], recv1.at[10], "gy", False),
        Shift(pz, pz_lo, send1.at[11], recv1.at[11], "gz", True),
        Shift(pz, pz_hi, send1.at[12], recv1.at[12], "gz", False),
    ]
    for copy in round1:
        copy.wait_recv()
    sent = round1 + later

    def mix(lo, hi):
        return jnp.where(even, roll(hi, NZL - 1, 1), roll(lo, 1, 1))

    zmix[0] = mix(zin_lo[0], zin_hi[0])
    zmix[2] = mix(zin_lo[1], zin_hi[1])
    for x in range(NXL):
        row = pl.ds(x, 1)
        fc[x + 1, pl.ds(TOP - 1, 1)] = yup_in[0, row]
        fu1[x + 1, pl.ds(TOP - 1, 1)] = yup_in[1, row]
        fc[x + 1, pl.ds(LAST + 1, 1)] = ydn_in[row]

    wx[0] = 0.5 * (fc[0, inner] + fc[1, inner])

    def faces(i, x, k, value):
        if k == 0:
            vydn[i, pl.ds(x, 1)] = value[0:1]
        if k == BLOCKS - 1:
            vyup[i, pl.ds(x, 1)] = value[7:8]

    def start(x, carry):
        packed, pw, g0 = carry
        for k in range(BLOCKS):
            r = TOP + 8 * k
            rows, own = pl.ds(r, 8), pl.ds(8 * k, 8)
            c = fc[x + 1, rows]
            edge = place(x, k, zmix[0])
            xu = 0.5 * (c + fc[x + 2, rows])
            xd = wx[x, own]
            yu = 0.5 * (c + fc[x + 1, pl.ds(r + 1, 8)])
            yd = 0.5 * (c + fc[x + 1, pl.ds(r - 1, 8)])
            zu = 0.5 * (c + above(c, edge))
            zd = 0.5 * (c + below(c, edge))
            m = 1.0 / ((xd + xu) + (yd + yu) + (zd + zu))
            u2 = fu2[x + 1, rows]
            r0 = (
                (xu * fu0[x + 1, rows] - xd * fu0[x, rows])
                + (yu * fu1[x + 1, rows] - yd * fu1[x + 1, pl.ds(r - 1, 8)])
                + (zu * u2 - zd * below(u2, place(x, k, zmix[2])))
            )
            v = m * r0
            wx[x + 1, own] = xu
            wyu[x, own] = yu
            wyd[x, own] = yd
            wzu[x, own] = zu
            wzd[x, own] = zd
            minv[x, own] = m
            rhs[x, own] = r0
            zb = jnp.where(first, zd, jnp.where(final, zu, 0.0))
            wzb[x, own] = zb
            pw = pick(x, k, zb, pw)
            if k == 0:
                wyb[0, pl.ds(x, 1)] = yd[0:1]
            if k == BLOCKS - 1:
                wyb[1, pl.ds(x, 1)] = yu[7:8]
            fv0[x + 1, rows] = v
            packed = pick(x, k, v, packed)
            faces(0, x, k, v)
            g0 = g0 + v * r0
        return packed, pw, g0

    packed, pw, g0 = lax.fori_loop(0, NXL, start, (zero,) * 3, unroll=4)

    def exchange(i, field, packed):
        vz[i] = packed
        copies = [
            Shift(field.at[NXL, inner], vx_in.at[i, 0], sendv.at[i, 0], recvv.at[i, 0], "gx", True),
            Shift(field.at[1, inner], vx_in.at[i, 1], sendv.at[i, 1], recvv.at[i, 1], "gx", False),
            Shift(vyup.at[i], vy_in.at[i, 0], sendv.at[i, 2], recvv.at[i, 2], "gy", True),
            Shift(vydn.at[i], vy_in.at[i, 1], sendv.at[i, 3], recvv.at[i, 3], "gy", False),
            Shift(vz.at[i], vz_lo.at[i], sendv.at[i, 4], recvv.at[i, 4], "gz", True),
            Shift(vz.at[i], vz_hi.at[i], sendv.at[i, 5], recvv.at[i, 5], "gz", False),
        ]
        for copy in copies:
            copy.start()
        if i == 0:
            for copy in later:
                copy.start()
        sent.extend(copies)
        heard(i)
        if i < 2:
            tell(i + 1)
        else:
            for d in range(1, RING):
                pl.semaphore_signal(
                    ready, inc=1, device_id={"gz": lax.rem(pos["gz"] + d, RING)}, device_id_type=MESH
                )
        return copies

    def interior(i, field):
        def plane_of(x, dot):
            for k in range(BLOCKS):
                r = TOP + 8 * k
                rows, own = pl.ds(r, 8), pl.ds(8 * k, 8)
                v = field[x + 1, rows]
                q = (
                    (wx[x, own] * (v - field[x, rows]) + wx[x + 1, own] * (v - field[x + 2, rows]))
                    + (
                        wyd[x, own] * (v - field[x + 1, pl.ds(r - 1, 8)])
                        + wyu[x, own] * (v - field[x + 1, pl.ds(r + 1, 8)])
                    )
                    + (wzd[x, own] * (v - below(v, 0.0)) + wzu[x, own] * (v - above(v, 0.0)))
                )
                part[x, own] = q
                dot = dot + v * q
            return dot

        return lax.fori_loop(0, NXL, plane_of, zero, unroll=4)

    def arrive(i, copies):
        for copy in copies:
            copy.wait_recv()
        vmix[i] = mix(vz_lo[i], vz_hi[i])

    def join(i):
        part[0] = part[0] - wx[0] * vx_in[i, 0]
        part[NXL - 1] = part[NXL - 1] - wx[NXL] * vx_in[i, 1]
        for x in range(NXL):
            row = pl.ds(x, 1)
            part[x, 0:1] = part[x, 0:1] - wyb[0, row] * vy_in[i, 0, row]
            part[x, NYL - 1 : NYL] = part[x, NYL - 1 : NYL] - wyb[1, row] * vy_in[i, 1, row]

    def around(x, k, i, field):
        r = TOP + 8 * k
        rows = pl.ds(r, 8)
        v = field[x + 1, rows]
        edge = place(x, k, vmix[i])
        return (
            v,
            (field[x + 2, rows], field[x + 1, pl.ds(r + 1, 8)], above(v, edge)),
            (field[x, rows], field[x + 1, pl.ds(r - 1, 8)], below(v, edge)),
        )

    copies = exchange(0, fv0, packed)
    interior(0, fv0)
    arrive(0, copies)
    join(0)

    def step0(x, carry):
        packed, h00, h01 = carry
        for k in range(BLOCKS):
            own, rows = pl.ds(8 * k, 8), pl.ds(TOP + 8 * k, 8)
            v = fv0[x + 1, rows]
            q = part[x, own] - wzb[x, own] * place(x, k, vmix[0])
            w = minv[x, own] * q - v
            img[x, own] = q
            fv1[x + 1, rows] = w
            packed = pick(x, k, w, packed)
            faces(1, x, k, w)
            h00 = h00 + v * q
            h01 = h01 + w * q
        return packed, h00, h01

    packed, h00, h01 = lax.fori_loop(0, NXL, step0, (zero, zero, zero), unroll=4)
    copies = exchange(1, fv1, packed)
    interior(1, fv1)
    arrive(1, copies)
    join(1)

    def step1(x, carry):
        packed, h11, h12 = carry
        for k in range(BLOCKS):
            own, rows = pl.ds(8 * k, 8), pl.ds(TOP + 8 * k, 8)
            v = fv1[x + 1, rows]
            q = part[x, own] - wzb[x, own] * place(x, k, vmix[1])
            w = minv[x, own] * q - v
            fv2[x + 1, rows] = w
            packed = pick(x, k, w, packed)
            faces(2, x, k, w)
            h11 = h11 + v * q
            h12 = h12 + w * q
        return packed, h11, h12

    packed, h11, h12 = lax.fori_loop(0, NXL, step1, (zero,) * 3, unroll=4)
    copies = exchange(2, fv2, packed)
    inside = interior(2, fv2)

    def dots(x, carry):
        h02, g2 = carry
        for k in range(BLOCKS):
            own = pl.ds(8 * k, 8)
            v = fv2[x + 1, pl.ds(TOP + 8 * k, 8)]
            h02 = h02 + v * img[x, own]
            g2 = g2 + v * rhs[x, own]
        return h02, g2

    h02, g2 = lax.fori_loop(0, NXL, dots, (zero, zero), unroll=4)
    arrive(2, copies)
    outside = pw * packed * vmix[2]
    for k in range(BLOCKS):
        own, rows = pl.ds(8 * k, 8), pl.ds(TOP + 8 * k, 8)
        outside = outside + (
            wx[0, own] * fv2[1, rows] * vx_in[2, 0, own] + wx[NXL, own] * fv2[NXL, rows] * vx_in[2, 1, own]
        )
    for half_x in range(NXL // 8):
        xs = pl.ds(8 * half_x, 8)
        outside = outside + (
            wyb[0, xs] * vydn[2, xs] * vy_in[2, 0, xs] + wyb[1, xs] * vyup[2, xs] * vy_in[2, 1, xs]
        )
    h22 = inside - outside

    sub = lax.broadcasted_iota(jnp.int32, (8, NZL), 0)
    level = [(value, None) for value in (g0, g2, h00, h01, h02, h11, h12, h22)]
    for width in (4, 2, 1):
        keep = lax.rem(sub // width, 2) == 0
        merged = []
        n = len(level) // 2
        for i in range(n):
            (ah, al), (bh, bl) = level[i], level[i + n]
            hi, err = two_sum(jnp.where(keep, ah, bh), roll_rows(jnp.where(keep, bh, ah), width, keep))
            if al is not None:
                err = err + (jnp.where(keep, al, bl) + roll_rows(jnp.where(keep, bl, al), width, keep))
            merged.append((hi, err))
        level = merged
    hi, lo = level[0]
    for width in (64, 32, 16, 8, 4, 2, 1):
        hi, err = two_sum(hi, roll(hi, width, 1))
        lo = (lo + roll(lo, width, 1)) + err
    own_row = jnp.where(lane == sub, hi, 0.0) + jnp.where(lane == sub + 64, lo, 0.0)
    row = jnp.sum(own_row, axis=0, keepdims=True)

    low_half = lax.broadcasted_iota(jnp.int32, (1, NZL), 1) < 64

    slot0 = 0
    drains = []
    for phase, axes in enumerate(PHASES):
        count = RING ** len(axes)
        mine = 0
        for axis in axes:
            mine = mine * RING + pos[axis]
        slots = sums.at[pl.ds(slot0, count)]
        slots[mine] = row
        if len(axes) > 1:
            pl.semaphore_wait(ready, RING - 1)
        offsets = [()]
        for axis in axes:
            offsets = [o + (d,) for o in offsets for d in range(RING)]
        offsets = sorted(offsets[1:], key=lambda o: -sum(min(d, RING - d) for d in o))
        for o in offsets:
            device = {axis: lax.rem(pos[axis] + d, RING) for axis, d in zip(axes, o) if d}
            remote(slots.at[mine], slots.at[mine], sendr.at[phase], recvr.at[phase], device).start()
        if phase == 0:
            for copy in later:
                copy.wait_recv()
            zmix[1] = mix(pz_lo[...], pz_hi[...])
            for i, field in enumerate((fv0, fv1, fv2)):
                field[0, inner] = vx_in[i, 0]
                field[NXL + 1, inner] = vx_in[i, 1]
            for x in range(NXL):
                lrow = pl.ds(x, 1)
                fp[x + 1, pl.ds(TOP - 1, 1)] = pyup_in[lrow]
                fp[x + 1, pl.ds(LAST + 1, 1)] = pydn_in[lrow]
                for i, field in enumerate((fv0, fv1, fv2)):
                    field[x + 1, pl.ds(TOP - 1, 1)] = vy_in[i, 0, lrow]
                    field[x + 1, pl.ds(LAST + 1, 1)] = vy_in[i, 1, lrow]

            def terms(x, carry):
                for k in range(BLOCKS):
                    r = TOP + 8 * k
                    rows, own = pl.ds(r, 8), pl.ds(8 * k, 8)
                    p = fp[x + 1, rows]
                    pe = place(x, k, zmix[1])
                    gu = (
                        -0.5 * (fp[x + 2, rows] - p),
                        -0.5 * (fp[x + 1, pl.ds(r + 1, 8)] - p),
                        -0.5 * (above(p, pe) - p),
                    )
                    gd = (
                        -0.5 * (p - fp[x, rows]),
                        -0.5 * (p - fp[x + 1, pl.ds(r - 1, 8)]),
                        -0.5 * (p - below(p, pe)),
                    )
                    u2 = fu2[x + 1, rows]
                    bases[0, x, own] = (
                        (gd[0] * fu0[x, rows] + gu[0] * fu0[x + 1, rows])
                        + (gd[1] * fu1[x + 1, pl.ds(r - 1, 8)] + gu[1] * fu1[x + 1, rows])
                        + (gd[2] * below(u2, place(x, k, zmix[2])) + gu[2] * u2)
                    )
                    for i, field in enumerate((fv0, fv1, fv2)):
                        v, up, down = around(x, k, i, field)
                        total = None
                        for dim in range(3):
                            upper, lower = up[dim] - v, v - down[dim]
                            grads[i, dim, x, own] = upper
                            term = gd[dim] * lower + gu[dim] * upper
                            total = term if total is None else total + term
                        bases[1 + i, x, own] = total
                return carry

            lax.fori_loop(0, NXL, terms, 0)
        others = sums.at[pl.ds(slot0, count - 1)]
        pltpu.make_async_copy(others, others, recvr.at[phase]).wait()
        drains.append(pltpu.make_async_copy(others, others, sendr.at[phase]))
        parts = [sums[slot0 + i] for i in range(count)]
        errs = []
        while len(parts) > 1:
            pairs = [two_sum(parts[i], parts[i + 1]) for i in range(0, len(parts), 2)]
            parts = [s for s, _ in pairs]
            errs.append(sum_tree([e for _, e in pairs]))
        total, err = parts[0], sum_tree(errs)
        row = jnp.where(low_half, total, total + roll(err, 64, 1))
        slot0 += count

    spread = jnp.broadcast_to(row, (8, NZL))
    col_hi = jnp.sum(jnp.where(lane == sub, spread, 0.0), axis=1, keepdims=True)
    col_lo = jnp.sum(jnp.where(lane == sub + 64, spread, 0.0), axis=1, keepdims=True)
    col_hi = jnp.broadcast_to(col_hi, (8, NZL))
    col_lo = jnp.broadcast_to(col_lo, (8, NZL))
    order = ROW_OF
    sums_hi_lo = [(col_hi[order[i] : order[i] + 1], col_lo[order[i] : order[i] + 1]) for i in range(8)]
    y = [jnp.broadcast_to(value, (8, NZL)) for value in galerkin(sums_hi_lo)]

    def finish(x, carry):
        for k in range(BLOCKS):
            rows, own = pl.ds(TOP + 8 * k, 8), pl.ds(8 * k, 8)
            for dim, field in enumerate((fu0, fu1, fu2)):
                grad = y[0] * grads[0, dim, x, own] + y[1] * grads[1, dim, x, own] + y[2] * grads[2, dim, x, own]
                out_u[dim, x, own] = field[x + 1, rows] + grad
            out_c[x, own] = bases[0, x, own] + (
                y[0] * bases[1, x, own] + y[1] * bases[2, x, own] + y[2] * bases[3, x, own]
            )
        return carry

    lax.fori_loop(0, NXL, finish, 0, unroll=4)
    for drain in drains:
        drain.wait()
    for copy in sent:
        copy.wait_send()


def roll_rows(x, width, keep):
    if width == 4:
        return roll(x, 4, 0)
    return jnp.where(keep, roll(x, 8 - width, 0), roll(x, width, 0))


def sum_tree(values):
    total = values[0]
    for value in values[1:]:
        total = total + value
    return total


def row_order():
    level = [{i: set(range(8))} for i in range(8)]
    names = [[i] * 8 for i in range(8)]
    for width in (4, 2, 1):
        n = len(names) // 2
        names = [
            [names[i][r] if (r // width) % 2 == 0 else names[i + n][r] for r in range(8)] for i in range(n)
        ]
    return [names[0].index(i) for i in range(8)]


ROW_OF = row_order()


def save(ustar, coef, ustar_hbm, coef_hbm, sem):
    stores = [
        pltpu.make_async_copy(ustar, ustar_hbm, sem.at[0]),
        pltpu.make_async_copy(coef, coef_hbm, sem.at[1]),
    ]
    for store in stores:
        store.start()
    for store in stores:
        store.wait()


def on_device(phase_mask, pressure, velocity_cot):
    field = pltpu.VMEM((NXL + 2, 48, NZL), F32)
    block = pltpu.VMEM((NXL, NYL, NZL), F32)
    flat = pltpu.VMEM((NXL, NZL), F32)
    flats = pltpu.VMEM((3, NXL, NZL), F32)
    tile = pltpu.VMEM((8, NZL), F32)
    tiles = pltpu.VMEM((3, 8, NZL), F32)
    dma = pltpu.SemaphoreType.DMA
    in_hbm = pl.BlockSpec(memory_space=pltpu.HBM)
    in_vmem = pl.BlockSpec(memory_space=pltpu.VMEM)
    out_shape = (
        jax.ShapeDtypeStruct((3, NXL, NYL, NZL), F32),
        jax.ShapeDtypeStruct((NXL, NYL, NZL), F32),
    )
    inputs = [
        pltpu.with_memory_space_constraint(a, pltpu.HBM) for a in (phase_mask, pressure, velocity_cot)
    ]
    outs = pl.pallas_call(
        body,
        out_shape=out_shape,
        in_specs=[in_hbm] * 3,
        out_specs=(in_vmem, in_vmem),
        scratch_shapes=[
            pltpu.VMEM((NXL, NYL, NZL), jnp.int32),
            *[field] * 8,
            pltpu.VMEM((NXL + 1, NYL, NZL), F32),
            *[block] * 5,
            pltpu.VMEM((2, NXL, NZL), F32),
            *[block] * 4,
            pltpu.VMEM((3, 3, NXL, NYL, NZL), F32),
            pltpu.VMEM((4, NXL, NYL, NZL), F32),
            pltpu.VMEM((2, NXL, NZL), F32), flat, pltpu.VMEM((2, NXL, NZL), F32), flat,
            *[flat] * 4,
            *[flats] * 2,
            pltpu.VMEM((3, 2, NXL, NZL), F32),
            pltpu.VMEM((3, 2, NYL, NZL), F32),
            *[pltpu.VMEM((2, 8, NZL), F32)] * 3,
            *[tile] * 3,
            *[tiles] * 5,
            pltpu.VMEM((sum(RING ** len(axes) for axes in PHASES), 1, NZL), F32),
            dma((5,)),
            dma((13,)), dma((13,)), dma((3, 6)), dma((3, 6)),
            dma((len(PHASES),)), dma((len(PHASES),)),
            pltpu.SemaphoreType.REGULAR,
            pltpu.SemaphoreType.REGULAR((3, 3)),
        ],
        compiler_params=pltpu.CompilerParams(
            collective_id=0, has_side_effects=True, vmem_limit_bytes=24 * 1024 * 1024
        ),
        name="projection_adjoint",
    )(*inputs)
    return pl.pallas_call(
        save,
        out_shape=out_shape,
        in_specs=[in_vmem] * 2,
        out_specs=(in_hbm, in_hbm),
        scratch_shapes=[dma((2,))],
        compiler_params=pltpu.CompilerParams(vmem_limit_bytes=4 * 1024 * 1024),
        name="save",
    )(*outs)


def solution(mesh):
    in_specs = (P("gx", "gy", "gz"), P("gx", "gy", "gz"), P(None, "gx", "gy", "gz"))
    out_specs = (P(None, "gx", "gy", "gz"), P("gx", "gy", "gz"))
    return jax.shard_map(
        on_device, mesh=mesh, in_specs=in_specs, out_specs=out_specs, check_vma=False
    )
```

```python
import jax
import jax.numpy as jnp
from jax import lax
from jax.experimental import pallas as pl
from jax.experimental.pallas import tpu as pltpu
from jax.sharding import PartitionSpec as P


MESH = pl.DeviceIdType.MESH
AXES = ("gx", "gy", "gz")
RING = 8
NXL, NYL, NZL = 16, 32, 128
TOP = 8
LAST = TOP + NYL - 1
BLOCKS = NYL // 8
F32 = jnp.float32
PHASES = (("gy",), ("gx", "gz"))


def two_sum(a, b):
    s = a + b
    t = s - a
    return s, (a - (s - t)) + (b - t)


def split(a):
    c = 4097.0 * a
    hi = c - (c - a)
    return hi, a - hi


def sub_mul(x, c, y):
    p = c * y[0]
    ch, cl = split(c)
    yh, yl = split(y[0])
    err = ((ch * yh - p) + ch * yl + cl * yh) + cl * yl
    s, t = two_sum(x[0], -p)
    t = t + (x[1] - (err + c * y[1]))
    hi = s + t
    return hi, t - (hi - s)


def galerkin(sums):
    g0, g2, h00, h01, h02, h11, h12, h22 = sums
    one = jnp.ones_like(g0[0])
    g1 = sub_mul(h00, one, g0)
    a = h01[0] / h00[0]
    b = h02[0] / h00[0]
    h01p = sub_mul(h01, a, h00)
    h02p = sub_mul(h02, b, h00)
    h11p = sub_mul(sub_mul(h11, a, h01), a, h01p)
    h12p = sub_mul(sub_mul(h12, a, h02), b, h01p)
    h22p = sub_mul(sub_mul(h22, b, h02), b, h02p)
    g1p = sub_mul(g1, a, g0)
    g2p = sub_mul(g2, b, g0)
    ok1 = h11p[0] > 1e-10 * h11[0]
    inv1 = jnp.where(ok1, 1.0 / jnp.where(ok1, h11p[0], 1.0), 0.0)
    c = h12p[0] * inv1
    h12q = sub_mul(h12p, c, h11p)
    h22q = sub_mul(sub_mul(h22p, c, h12p), c, h12q)
    g2q = sub_mul(g2p, c, g1p)
    h02q = h02p[0] - c * h01p[0]
    ok2 = h22q[0] > 1e-10 * h22[0]
    y2 = jnp.where(ok2, g2q[0] / jnp.where(ok2, h22q[0], 1.0), 0.0)
    y1p = (g1p[0] - h12q[0] * y2) * inv1
    y0p = (g0[0] - h01p[0] * y1p - h02q * y2) / h00[0]
    return y0p - a * y1p - (b - c * a) * y2, y1p - c * y2, y2


def roll(x, shift, axis):
    return pltpu.roll(x, shift, axis)


def remote(src, dst, send, recv, device):
    return pltpu.make_async_remote_copy(
        src_ref=src, dst_ref=dst, send_sem=send, recv_sem=recv, device_id=device, device_id_type=MESH
    )


def body(
    mask_hbm, press_hbm, vel_hbm, out_u, out_c,
    mask, fc, fp, fu0, fu1, fu2, fv0, fv1, fv2,
    wx, wyu, wyd, wzu, wzd, wyb, minv, rhs, img, part,
    grads, bases,
    kx_out, kx_in, ky_out, ky_in, kz_out, kz_lo, kz_hi,
    tx_out, tx_in, ty_out, ty_in, tz_out, tz_lo, tz_hi,
    dxy, dxz, dyz, dyz_rows,
    cyup, cydn, uyup, cx_in, ux_in, cy_in, uy_in, pyup, pydn, pyup_in, pydn_in, vyup, vydn, vy_in, vx_in,
    cz, cz_lo, cz_hi, uz, uz_lo, pz, pz_lo, pz_hi, zmix, vz, vz_lo, vz_hi, vmix,
    sums,
    load_sem,
    send1, recv1, sendv, recvv, sendr, recvr, ready, token, sendk, recvk,
):
    pos = {axis: lax.axis_index(axis) for axis in AXES}
    fwd = {axis: lax.rem(pos[axis] + 1, RING) for axis in AXES}
    bwd = {axis: lax.rem(pos[axis] + RING - 1, RING) for axis in AXES}
    lane = lax.broadcasted_iota(jnp.int32, (8, NZL), 1)
    sub = lax.broadcasted_iota(jnp.int32, (8, NZL), 0)
    half = lane // 2
    even = lane - 2 * half == 0
    first = lane == 0
    final = lane == NZL - 1
    border = jnp.logical_or(first, final)

    low = {axis: pos[axis] == 0 for axis in AXES}
    high = {axis: pos[axis] == RING - 1 for axis in AXES}

    class Shift:
        def __init__(self, src, dst, send, recv, *moves):
            moves = tuple(zip(moves[::2], moves[1::2]))
            device = {axis: fwd[axis] if up else bwd[axis] for axis, up in moves}
            self.copy = remote(src, dst, send, recv, device)
            self.sends = self.receives = None
            for axis, up in moves:
                sends = jnp.logical_not(high[axis] if up else low[axis])
                receives = jnp.logical_not(low[axis] if up else high[axis])
                self.sends = sends if self.sends is None else jnp.logical_and(self.sends, sends)
                self.receives = receives if self.receives is None else jnp.logical_and(self.receives, receives)

        def start(self):
            pl.when(self.sends)(lambda: self.copy.start())

        def wait_recv(self):
            pl.when(self.receives)(lambda: self.copy.wait_recv())

        def wait_send(self):
            pl.when(self.sends)(lambda: self.copy.wait_send())

    def tell(stage):
        for a, axis in enumerate(AXES):
            for end, other in ((high[axis], fwd[axis]), (low[axis], bwd[axis])):

                @pl.when(end)
                def _(a=a, axis=axis, other=other):
                    pl.semaphore_signal(
                        token.at[stage, a], inc=1, device_id={axis: other}, device_id_type=MESH
                    )

    def heard(stage):
        for a, axis in enumerate(AXES):

            @pl.when(jnp.logical_or(high[axis], low[axis]))
            def _(a=a):
                pl.semaphore_wait(token.at[stage, a], 1)

    cells = (pl.ds(1, NXL), pl.ds(TOP, NYL))
    loads = [pltpu.make_async_copy(mask_hbm, mask, load_sem.at[0])]
    for i, field in ((2, fu2), (1, fu1), (0, fu0)):
        loads.append(pltpu.make_async_copy(vel_hbm.at[i], field.at[cells], load_sem.at[1 + i]))
    loads.append(pltpu.make_async_copy(press_hbm, fp.at[cells], load_sem.at[4]))
    for load in loads:
        load.start()

    inner = pl.ds(TOP, NYL)
    plane = jnp.zeros((NYL, NZL), F32)
    line = jnp.zeros((1, NZL), F32)
    zero = jnp.zeros((8, NZL), F32)
    for field in (fc, fp, fu0, fv0, fv1, fv2):
        field[0, inner] = plane
        field[NXL + 1, inner] = plane
    for x in range(1, NXL + 1):
        fu1[x, pl.ds(TOP - 1, 1)] = line
        for field in (fc, fv0, fv1, fv2):
            field[x, pl.ds(TOP - 1, 1)] = line
            field[x, pl.ds(LAST + 1, 1)] = line
    for buffer in (
        cx_in, ux_in, cy_in, uy_in, pyup_in, pydn_in, vy_in, vx_in,
        cz_lo, cz_hi, uz_lo, pz_lo, pz_hi, vz_lo, vz_hi,
        kx_in, ky_in, kz_lo, kz_hi, tx_in, ty_in, tz_lo, tz_hi, dxy, dxz, dyz, dyz_rows, kx_out, ky_out,
    ):
        buffer[...] = jnp.zeros(buffer.shape, F32)

    barrier = pltpu.get_barrier_semaphore()
    for axis in AXES:
        for other in (fwd[axis], bwd[axis]):
            pl.semaphore_signal(barrier, inc=1, device_id={axis: other}, device_id_type=MESH)
    def pick(x, k, value, packed):
        return jnp.where(half == BLOCKS * x + k, roll(value, 2 * BLOCKS * x + 2 * k + 1, 1), packed)

    def place(x, k, mixed):
        return roll(mixed, NZL - 1 - 2 * BLOCKS * x - 2 * k, 1)

    def above(value, edge):
        return jnp.where(final, edge, roll(value, NZL - 1, 1))

    def below(value, edge):
        return jnp.where(first, edge, roll(value, 1, 1))

    loads[0].wait()

    def prepare(x, packed):
        for k in range(BLOCKS):
            phase = mask[x, pl.ds(8 * k, 8)]
            c = jnp.where(phase == 0, 8.0, jnp.where(phase == 1, 1.0, 2.0)).astype(F32)
            fc[x + 1, pl.ds(TOP + 8 * k, 8)] = c
            packed = pick(x, k, c, packed)
            if k == 0:
                cydn[pl.ds(x, 1)] = c[0:1]
            if k == BLOCKS - 1:
                cyup[pl.ds(x, 1)] = c[7:8]
        return packed

    cz[...] = lax.fori_loop(0, NXL, prepare, zero, unroll=4)
    pl.semaphore_wait(barrier, 6)
    sent = []

    def launch(copies):
        for copy in copies:
            copy.start()
        sent.extend(copies)
        return copies

    round1 = launch([
        Shift(fc.at[NXL, inner], cx_in.at[0], send1.at[0], recv1.at[0], "gx", True),
        Shift(fc.at[1, inner], cx_in.at[1], send1.at[1], recv1.at[1], "gx", False),
        Shift(cyup, cy_in.at[0], send1.at[2], recv1.at[2], "gy", True),
        Shift(cydn, cy_in.at[1], send1.at[3], recv1.at[3], "gy", False),
        Shift(cz, cz_lo, send1.at[4], recv1.at[4], "gz", True),
        Shift(cz, cz_hi, send1.at[5], recv1.at[5], "gz", False),
    ])
    for load in loads[1:4]:
        load.wait()

    def velocity(x, packed):
        for k in range(BLOCKS):
            packed = pick(x, k, fu2[x + 1, pl.ds(TOP + 8 * k, 8)], packed)
        uyup[pl.ds(x, 1)] = fu1[x + 1, pl.ds(LAST, 1)]
        return packed

    uz[...] = lax.fori_loop(0, NXL, velocity, zero, unroll=4)
    round1 += launch([
        Shift(uz, uz_lo, send1.at[6], recv1.at[6], "gz", True),
        Shift(fu0.at[NXL, inner], ux_in, send1.at[7], recv1.at[7], "gx", True),
        Shift(uyup, uy_in, send1.at[8], recv1.at[8], "gy", True),
    ])
    tell(0)
    loads[4].wait()

    def mix(lo, hi):
        return jnp.where(even, roll(hi, NZL - 1, 1), roll(lo, 1, 1))

    def weigh(x, carry):
        pw, pp = carry
        for k in range(BLOCKS):
            r = TOP + 8 * k
            rows, own = pl.ds(r, 8), pl.ds(8 * k, 8)
            c = fc[x + 1, rows]
            xu = 0.5 * (c + fc[x + 2, rows])
            xd = 0.5 * (c + fc[x, rows])
            yu = 0.5 * (c + fc[x + 1, pl.ds(r + 1, 8)])
            yd = 0.5 * (c + fc[x + 1, pl.ds(r - 1, 8)])
            zu = 0.5 * (c + above(c, 0.0))
            zd = 0.5 * (c + below(c, 0.0))
            u2 = fu2[x + 1, rows]
            wx[x + 1, own] = xu
            wyu[x, own] = yu
            wyd[x, own] = yd
            wzu[x, own] = zu
            wzd[x, own] = zd
            minv[x, own] = (xd + xu) + (yd + yu) + (zd + zu)
            rhs[x, own] = (
                (xu * fu0[x + 1, rows] - xd * fu0[x, rows])
                + (yu * fu1[x + 1, rows] - yd * fu1[x + 1, pl.ds(r - 1, 8)])
                + (zu * u2 - zd * below(u2, 0.0))
            )
            pw = pick(x, k, jnp.where(first, zd, zu), pw)
            p = fp[x + 1, rows]
            pp = pick(x, k, p, pp)
            if k == 0:
                pydn[pl.ds(x, 1)] = p[0:1]
            if k == BLOCKS - 1:
                pyup[pl.ds(x, 1)] = p[7:8]
        return pw, pp

    pw, pp = lax.fori_loop(0, NXL, weigh, (zero, zero), unroll=4)
    pz[...] = pp
    later = [
        Shift(fp.at[NXL, inner], fp.at[0, inner], send1.at[9], recv1.at[9], "gx", True),
        Shift(fp.at[1, inner], fp.at[NXL + 1, inner], send1.at[10], recv1.at[10], "gx", False),
        Shift(pyup, pyup_in, send1.at[11], recv1.at[11], "gy", True),
        Shift(pydn, pydn_in, send1.at[12], recv1.at[12], "gy", False),
        Shift(pz, pz_lo, send1.at[13], recv1.at[13], "gz", True),
        Shift(pz, pz_hi, send1.at[14], recv1.at[14], "gz", False),
    ]
    for copy in round1:
        copy.wait_recv()

    h = 0.5 * cx_in[0]
    w = 0.5 * fc[1, inner] + h
    wx[0] = w
    minv[0] = minv[0] + h
    rhs[0] = rhs[0] - w * ux_in[...]
    h = 0.5 * cx_in[1]
    wx[NXL] = wx[NXL] + h
    minv[NXL - 1] = minv[NXL - 1] + h
    rhs[NXL - 1] = rhs[NXL - 1] + h * fu0[NXL, inner]
    for x in range(NXL):
        row, top, bottom = pl.ds(x, 1), pl.ds(0, 1), pl.ds(NYL - 1, 1)
        h = 0.5 * cy_in[0, row]
        w = wyd[x, top] + h
        wyd[x, top] = w
        wyb[0, row] = w
        minv[x, top] = minv[x, top] + h
        rhs[x, top] = rhs[x, top] - w * uy_in[row]
        h = 0.5 * cy_in[1, row]
        w = wyu[x, bottom] + h
        wyu[x, bottom] = w
        wyb[1, row] = w
        minv[x, bottom] = minv[x, bottom] + h
        rhs[x, bottom] = rhs[x, bottom] + h * uyup[row]
    hz = 0.5 * mix(cz_lo[...], cz_hi[...])
    pw = pw + hz
    uz_mix = roll(uz_lo[...], 1, 1)
    zmix[1] = uz_mix
    pr = jnp.where(even, hz * uz[...], -pw * uz_mix)

    def faces(i, x, k, value):
        if k == 0:
            vydn[i, pl.ds(x, 1)] = value[0:1]
        if k == BLOCKS - 1:
            vyup[i, pl.ds(x, 1)] = value[7:8]

    def start(x, carry):
        packed, g0 = carry
        for k in range(BLOCKS):
            own = pl.ds(8 * k, 8)
            m = 1.0 / (minv[x, own] + jnp.where(border, place(x, k, hz), 0.0))
            r0 = rhs[x, own] + jnp.where(border, place(x, k, pr), 0.0)
            v = m * r0
            minv[x, own] = m
            rhs[x, own] = r0
            fv0[x + 1, pl.ds(TOP + 8 * k, 8)] = v
            packed = pick(x, k, v, packed)
            faces(0, x, k, v)
            g0 = g0 + v * r0
        return packed, g0

    packed, g0 = lax.fori_loop(0, NXL, start, (zero,) * 2, unroll=4)

    def exchange(i, field, packed):
        vz[i] = packed
        copies = [
            Shift(field.at[NXL, inner], vx_in.at[i, 0], sendv.at[i, 0], recvv.at[i, 0], "gx", True),
            Shift(field.at[1, inner], vx_in.at[i, 1], sendv.at[i, 1], recvv.at[i, 1], "gx", False),
            Shift(vyup.at[i], vy_in.at[i, 0], sendv.at[i, 2], recvv.at[i, 2], "gy", True),
            Shift(vydn.at[i], vy_in.at[i, 1], sendv.at[i, 3], recvv.at[i, 3], "gy", False),
            Shift(vz.at[i], vz_lo.at[i], sendv.at[i, 4], recvv.at[i, 4], "gz", True),
            Shift(vz.at[i], vz_hi.at[i], sendv.at[i, 5], recvv.at[i, 5], "gz", False),
        ]
        launch(copies)
        if i == 0:
            launch(later)
        heard(i)
        tell(i + 1)
        return copies

    def interior(i, field):
        def plane_of(x, carry):
            dot, packed = carry
            for k in range(BLOCKS):
                r = TOP + 8 * k
                rows, own = pl.ds(r, 8), pl.ds(8 * k, 8)
                v = field[x + 1, rows]
                q = (
                    (wx[x, own] * (v - field[x, rows]) + wx[x + 1, own] * (v - field[x + 2, rows]))
                    + (
                        wyd[x, own] * (v - field[x + 1, pl.ds(r - 1, 8)])
                        + wyu[x, own] * (v - field[x + 1, pl.ds(r + 1, 8)])
                    )
                    + (wzd[x, own] * (v - below(v, 0.0)) + wzu[x, own] * (v - above(v, 0.0)))
                )
                part[x, own] = q
                if i == 1:
                    packed = pick(x, k, q, packed)
                if i == 2:
                    dot = dot + v * q
            return dot, packed

        return lax.fori_loop(0, NXL, plane_of, (zero, zero), unroll=4)

    def arrive(i, copies):
        for copy in copies:
            copy.wait_recv()
        vmix[i] = mix(vz_lo[i], vz_hi[i])
        return pw * vmix[i] - hz * vz[i]

    def join(i):
        part[0] = part[0] - wx[0] * vx_in[i, 0]
        part[NXL - 1] = part[NXL - 1] - wx[NXL] * vx_in[i, 1]
        for x in range(NXL):
            row = pl.ds(x, 1)
            part[x, 0:1] = part[x, 0:1] - wyb[0, row] * vy_in[i, 0, row]
            part[x, NYL - 1 : NYL] = part[x, NYL - 1 : NYL] - wyb[1, row] * vy_in[i, 1, row]

    def around(x, k, i, field):
        r = TOP + 8 * k
        rows = pl.ds(r, 8)
        v = field[x + 1, rows]
        edge = place(x, k, vmix[i])
        return (
            v,
            (field[x + 2, rows], field[x + 1, pl.ds(r + 1, 8)], above(v, edge)),
            (field[x, rows], field[x + 1, pl.ds(r - 1, 8)], below(v, edge)),
        )

    copies = exchange(0, fv0, packed)
    interior(0, fv0)

    def at_border(x, k, mixed):
        return jnp.where(border, place(x, k, mixed), 0.0)

    def spread_rows(x, carry):
        pm, py = carry
        row = pl.ds(x, 1)
        for k in range(BLOCKS):
            own = pl.ds(8 * k, 8)
            m = minv[x, own]
            pm = pick(x, k, m, pm)
            if k == 0:
                py = pick(x, k, jnp.where(sub == 0, wyd[x, own], 0.0), py)
                ky_out[0, row] = m[0:1] * wyb[0, row]
                ky_out[0, pl.ds(NXL + x, 1)] = (m * at_border(x, k, pw))[0:1]
            if k == BLOCKS - 1:
                py = pick(x, k, jnp.where(sub == 7, wyu[x, own], 0.0), py)
                ky_out[1, row] = m[7:8] * wyb[1, row]
                ky_out[1, pl.ds(NXL + x, 1)] = (m * at_border(x, k, pw))[7:8]
        return pm, py

    pm, py = lax.fori_loop(0, NXL, spread_rows, (zero, zero))
    px = zero
    for side, p, wp in ((0, 0, 0), (1, NXL - 1, NXL)):
        for k in range(BLOCKS):
            own = pl.ds(8 * k, 8)
            px = pick(p, k, wx[wp, own], px)
            kx_out[side, own] = minv[p, own] * wx[wp, own]
            kx_out[side, pl.ds(NYL + 8 * k, 8)] = minv[p, own] * at_border(p, k, pw)
        for end, y in ((0, 0), (1, NYL - 1)):
            m = minv[p, pl.ds(y, 1)]
            kx_out[side, pl.ds(2 * NYL + end, 1)] = m * wyb[end, pl.ds(p, 1)]
            ky_out[end, pl.ds(2 * NXL + side, 1)] = m * wx[wp, pl.ds(y, 1)]
    kz_out[0] = pm * pw
    kz_out[1] = pm * px
    kz_out[2] = pm * py
    statics = launch([
        Shift(kx_out.at[1], kx_in.at[0], sendk.at[0], recvk.at[0], "gx", True),
        Shift(kx_out.at[0], kx_in.at[1], sendk.at[1], recvk.at[1], "gx", False),
        Shift(ky_out.at[1], ky_in.at[0], sendk.at[2], recvk.at[2], "gy", True),
        Shift(ky_out.at[0], ky_in.at[1], sendk.at[3], recvk.at[3], "gy", False),
        Shift(kz_out, kz_lo, sendk.at[4], recvk.at[4], "gz", True),
        Shift(kz_out, kz_hi, sendk.at[5], recvk.at[5], "gz", False),
    ])
    pq = arrive(0, copies)
    join(0)

    def step0(x, carry):
        packed, h00, h01 = carry
        for k in range(BLOCKS):
            own, rows = pl.ds(8 * k, 8), pl.ds(TOP + 8 * k, 8)
            v = fv0[x + 1, rows]
            q = part[x, own] - jnp.where(border, place(x, k, pq), 0.0)
            w = minv[x, own] * q - v
            img[x, own] = q
            fv1[x + 1, rows] = w
            packed = pick(x, k, w, packed)
            faces(1, x, k, w)
            h00 = h00 + v * q
            h01 = h01 + w * q
        return packed, h00, h01

    packed, h00, h01 = lax.fori_loop(0, NXL, step0, (zero, zero, zero), unroll=4)
    copies = exchange(1, fv1, packed)
    diagonal = []
    n = 12
    for a, up_a in enumerate((True, False)):
        for b, up_b in enumerate((True, False)):
            slot = 2 * a + b
            rows_b = (vyup if up_b else vydn).at[1]
            rows_a = (vyup if up_a else vydn).at[1]
            for src, dst, moves in (
                (rows_b, dxy, ("gx", up_a, "gy", up_b)),
                (vz.at[1], dxz, ("gx", up_a, "gz", up_b)),
                (vz.at[1], dyz, ("gy", up_a, "gz", up_b)),
                (rows_a, dyz_rows, ("gy", up_a, "gz", up_b)),
            ):
                diagonal.append(Shift(src, dst.at[slot], sendk.at[n], recvk.at[n], *moves))
                n += 1
    launch(diagonal)
    _, packed_part = interior(1, fv1)
    hv = hz * vz[1]
    tz_out[...] = pm * (packed_part + hv) - vz[1]
    for side, p in ((0, 0), (1, NXL - 1)):
        for k in range(BLOCKS):
            own = pl.ds(8 * k, 8)
            tx_out[side, own] = (
                minv[p, own] * (part[p, own] + at_border(p, k, hv)) - fv1[p + 1, pl.ds(TOP + 8 * k, 8)]
            )
    for x in range(NXL):
        row = pl.ds(x, 1)
        for side, k, y, r in ((0, 0, 0, 0), (1, BLOCKS - 1, NYL - 1, 7)):
            own = (vydn if side == 0 else vyup)[1, row]
            at = pl.ds(y, 1)
            ty_out[side, row] = minv[x, at] * (part[x, at] + at_border(x, k, hv)[r : r + 1]) - own
    partial = launch([
        Shift(tx_out.at[1], tx_in.at[0], sendk.at[6], recvk.at[6], "gx", True),
        Shift(tx_out.at[0], tx_in.at[1], sendk.at[7], recvk.at[7], "gx", False),
        Shift(ty_out.at[1], ty_in.at[0], sendk.at[8], recvk.at[8], "gy", True),
        Shift(ty_out.at[0], ty_in.at[1], sendk.at[9], recvk.at[9], "gy", False),
        Shift(tz_out, tz_lo, sendk.at[10], recvk.at[10], "gz", True),
        Shift(tz_out, tz_hi, sendk.at[11], recvk.at[11], "gz", False),
    ])
    pq = arrive(1, copies)
    join(1)

    def step1(x, carry):
        packed, h11, h12, h02, g2 = carry
        for k in range(BLOCKS):
            own, rows = pl.ds(8 * k, 8), pl.ds(TOP + 8 * k, 8)
            v = fv1[x + 1, rows]
            q = part[x, own] - jnp.where(border, place(x, k, pq), 0.0)
            w = minv[x, own] * q - v
            fv2[x + 1, rows] = w
            packed = pick(x, k, w, packed)
            faces(2, x, k, w)
            h11 = h11 + v * q
            h12 = h12 + w * q
            h02 = h02 + w * img[x, own]
            g2 = g2 + w * rhs[x, own]
        return packed, h11, h12, h02, g2

    packed, h11, h12, h02, g2 = lax.fori_loop(0, NXL, step1, (zero,) * 5, unroll=4)
    inside, _ = interior(2, fv2)
    heard(2)
    for d in range(1, RING):
        pl.semaphore_signal(
            ready, inc=1, device_id={"gz": lax.rem(pos["gz"] + d, RING)}, device_id_type=MESH
        )
    for copy in statics + partial + diagonal:
        copy.wait_recv()
    mixed_x = [mix(dxz[2 * side], dxz[2 * side + 1]) for side in (0, 1)]
    mixed_y = [mix(dyz[2 * side], dyz[2 * side + 1]) for side in (0, 1)]
    for side, p, mine in ((0, NXL - 1, 1), (1, 0, NXL)):
        for k in range(BLOCKS):
            own = pl.ds(8 * k, 8)
            vx_in[2, side, own] = (
                tx_in[side, own]
                - kx_in[side, own] * fv1[mine, pl.ds(TOP + 8 * k, 8)]
                - kx_in[side, pl.ds(NYL + 8 * k, 8)] * place(p, k, mixed_x[side])
            )
        for end, y in ((0, 0), (1, NYL - 1)):
            at = pl.ds(y, 1)
            vx_in[2, side, at] = vx_in[2, side, at] - (
                kx_in[side, pl.ds(2 * NYL + end, 1)] * dxy[2 * side + end, pl.ds(p, 1)]
            )
    for side in (0, 1):
        own_rows = vydn if side == 0 else vyup
        for block in range(NXL // 8):
            xs = pl.ds(8 * block, 8)
            beside = jnp.where(
                first, roll(dyz_rows[2 * side, xs], 1, 1), roll(dyz_rows[2 * side + 1, xs], NZL - 1, 1)
            )
            vy_in[2, side, xs] = (
                ty_in[side, xs]
                - ky_in[side, xs] * own_rows[1, xs]
                - ky_in[side, pl.ds(NXL + 8 * block, 8)] * beside
            )
        for end, x, far in ((0, 0, NXL - 1), (1, NXL - 1, 0)):
            at = pl.ds(x, 1)
            vy_in[2, side, at] = vy_in[2, side, at] - (
                ky_in[side, pl.ds(2 * NXL + end, 1)] * dxy[2 * end + side, pl.ds(far, 1)]
            )
    beside_x = jnp.where(lane < 64, roll(mixed_x[0], 2 * BLOCKS, 1), roll(mixed_x[1], NZL - 2 * BLOCKS, 1))
    step_k = 2 * (BLOCKS - 1)
    beside_y = jnp.where(
        sub == 0,
        roll(roll(mixed_y[0], NZL - step_k, 1), 1, 0),
        roll(roll(mixed_y[1], step_k, 1), 7, 0),
    )
    kz = [mix(kz_lo[i], kz_hi[i]) for i in range(3)]
    vmix[2] = (
        mix(tz_lo[...], tz_hi[...]) - kz[0] * vz[1] - kz[1] * beside_x - kz[2] * beside_y
    )
    pq = pw * vmix[2] - hz * packed
    outside = packed * pq
    for k in range(BLOCKS):
        own, rows = pl.ds(8 * k, 8), pl.ds(TOP + 8 * k, 8)
        outside = outside + (
            wx[0, own] * fv2[1, rows] * vx_in[2, 0, own] + wx[NXL, own] * fv2[NXL, rows] * vx_in[2, 1, own]
        )
    for half_x in range(NXL // 8):
        xs = pl.ds(8 * half_x, 8)
        outside = outside + (
            wyb[0, xs] * vydn[2, xs] * vy_in[2, 0, xs] + wyb[1, xs] * vyup[2, xs] * vy_in[2, 1, xs]
        )
    h22 = inside - outside

    level = [(value, None) for value in (g0, g2, h00, h01, h02, h11, h12, h22)]
    for width in (4, 2, 1):
        keep = lax.rem(sub // width, 2) == 0
        merged = []
        n = len(level) // 2
        for i in range(n):
            (ah, al), (bh, bl) = level[i], level[i + n]
            hi, err = two_sum(jnp.where(keep, ah, bh), roll_rows(jnp.where(keep, bh, ah), width, keep))
            if al is not None:
                err = err + (jnp.where(keep, al, bl) + roll_rows(jnp.where(keep, bl, al), width, keep))
            merged.append((hi, err))
        level = merged
    hi, lo = level[0]
    for width in (64, 32, 16, 8, 4, 2, 1):
        hi, err = two_sum(hi, roll(hi, width, 1))
        lo = (lo + roll(lo, width, 1)) + err
    own_row = jnp.where(lane == sub, hi, 0.0) + jnp.where(lane == sub + 64, lo, 0.0)
    row = jnp.sum(own_row, axis=0, keepdims=True)

    low_half = lax.broadcasted_iota(jnp.int32, (1, NZL), 1) < 64

    slot0 = 0
    drains = []
    for phase, axes in enumerate(PHASES):
        count = RING ** len(axes)
        mine = 0
        for axis in axes:
            mine = mine * RING + pos[axis]
        slots = sums.at[pl.ds(slot0, count)]
        slots[mine] = row
        if len(axes) > 1:
            pl.semaphore_wait(ready, RING - 1)
        offsets = [()]
        for axis in axes:
            offsets = [o + (d,) for o in offsets for d in range(RING)]
        offsets = sorted(offsets[1:], key=lambda o: -sum(min(d, RING - d) for d in o))
        for o in offsets:
            device = {axis: lax.rem(pos[axis] + d, RING) for axis, d in zip(axes, o) if d}
            remote(slots.at[mine], slots.at[mine], sendr.at[phase], recvr.at[phase], device).start()
        if phase == 0:
            for copy in later:
                copy.wait_recv()
            zmix[0] = mix(pz_lo[...], pz_hi[...])
            fu0[0, inner] = ux_in[...]
            for i, field in enumerate((fv0, fv1, fv2)):
                field[0, inner] = vx_in[i, 0]
                field[NXL + 1, inner] = vx_in[i, 1]
            for x in range(NXL):
                lrow = pl.ds(x, 1)
                fu1[x + 1, pl.ds(TOP - 1, 1)] = uy_in[lrow]
                fp[x + 1, pl.ds(TOP - 1, 1)] = pyup_in[lrow]
                fp[x + 1, pl.ds(LAST + 1, 1)] = pydn_in[lrow]
                for i, field in enumerate((fv0, fv1, fv2)):
                    field[x + 1, pl.ds(TOP - 1, 1)] = vy_in[i, 0, lrow]
                    field[x + 1, pl.ds(LAST + 1, 1)] = vy_in[i, 1, lrow]

            def terms(x, carry):
                for k in range(BLOCKS):
                    r = TOP + 8 * k
                    rows, own = pl.ds(r, 8), pl.ds(8 * k, 8)
                    p = fp[x + 1, rows]
                    pe = place(x, k, zmix[0])
                    gu = (
                        -0.5 * (fp[x + 2, rows] - p),
                        -0.5 * (fp[x + 1, pl.ds(r + 1, 8)] - p),
                        -0.5 * (above(p, pe) - p),
                    )
                    gd = (
                        -0.5 * (p - fp[x, rows]),
                        -0.5 * (p - fp[x + 1, pl.ds(r - 1, 8)]),
                        -0.5 * (p - below(p, pe)),
                    )
                    u2 = fu2[x + 1, rows]
                    bases[0, x, own] = (
                        (gd[0] * fu0[x, rows] + gu[0] * fu0[x + 1, rows])
                        + (gd[1] * fu1[x + 1, pl.ds(r - 1, 8)] + gu[1] * fu1[x + 1, rows])
                        + (gd[2] * below(u2, place(x, k, zmix[1])) + gu[2] * u2)
                    )
                    for i, field in enumerate((fv0, fv1, fv2)):
                        v, up, down = around(x, k, i, field)
                        total = None
                        for dim in range(3):
                            upper, lower = up[dim] - v, v - down[dim]
                            grads[i, dim, x, own] = upper
                            term = gd[dim] * lower + gu[dim] * upper
                            total = term if total is None else total + term
                        bases[1 + i, x, own] = total
                return carry

            lax.fori_loop(0, NXL, terms, 0)
        others = sums.at[pl.ds(slot0, count - 1)]
        pltpu.make_async_copy(others, others, recvr.at[phase]).wait()
        drains.append(pltpu.make_async_copy(others, others, sendr.at[phase]))
        parts = [sums[slot0 + i] for i in range(count)]
        errs = []
        while len(parts) > 1:
            pairs = [two_sum(parts[i], parts[i + 1]) for i in range(0, len(parts), 2)]
            parts = [s for s, _ in pairs]
            errs.append(sum_tree([e for _, e in pairs]))
        total, err = parts[0], sum_tree(errs)
        row = jnp.where(low_half, total, total + roll(err, 64, 1))
        slot0 += count

    spread = jnp.broadcast_to(row, (8, NZL))
    col_hi = jnp.sum(jnp.where(lane == sub, spread, 0.0), axis=1, keepdims=True)
    col_lo = jnp.sum(jnp.where(lane == sub + 64, spread, 0.0), axis=1, keepdims=True)
    col_hi = jnp.broadcast_to(col_hi, (8, NZL))
    col_lo = jnp.broadcast_to(col_lo, (8, NZL))
    order = ROW_OF
    sums_hi_lo = [(col_hi[order[i] : order[i] + 1], col_lo[order[i] : order[i] + 1]) for i in range(8)]
    y = [jnp.broadcast_to(value, (8, NZL)) for value in galerkin(sums_hi_lo)]

    def finish(x, carry):
        for k in range(BLOCKS):
            rows, own = pl.ds(TOP + 8 * k, 8), pl.ds(8 * k, 8)
            for dim, field in enumerate((fu0, fu1, fu2)):
                grad = y[0] * grads[0, dim, x, own] + y[1] * grads[1, dim, x, own] + y[2] * grads[2, dim, x, own]
                out_u[dim, x, own] = field[x + 1, rows] + grad
            out_c[x, own] = bases[0, x, own] + (
                y[0] * bases[1, x, own] + y[1] * bases[2, x, own] + y[2] * bases[3, x, own]
            )
        return carry

    lax.fori_loop(0, NXL, finish, 0, unroll=4)
    for drain in drains:
        drain.wait()
    for copy in sent:
        copy.wait_send()


def roll_rows(x, width, keep):
    if width == 4:
        return roll(x, 4, 0)
    return jnp.where(keep, roll(x, 8 - width, 0), roll(x, width, 0))


def sum_tree(values):
    total = values[0]
    for value in values[1:]:
        total = total + value
    return total


def row_order():
    level = [{i: set(range(8))} for i in range(8)]
    names = [[i] * 8 for i in range(8)]
    for width in (4, 2, 1):
        n = len(names) // 2
        names = [
            [names[i][r] if (r // width) % 2 == 0 else names[i + n][r] for r in range(8)] for i in range(n)
        ]
    return [names[0].index(i) for i in range(8)]


ROW_OF = row_order()


def save(ustar, coef, ustar_hbm, coef_hbm, sem):
    stores = [
        pltpu.make_async_copy(ustar, ustar_hbm, sem.at[0]),
        pltpu.make_async_copy(coef, coef_hbm, sem.at[1]),
    ]
    for store in stores:
        store.start()
    for store in stores:
        store.wait()


def on_device(phase_mask, pressure, velocity_cot):
    field = pltpu.VMEM((NXL + 2, 48, NZL), F32)
    block = pltpu.VMEM((NXL, NYL, NZL), F32)
    flat = pltpu.VMEM((NXL, NZL), F32)
    flats = pltpu.VMEM((3, NXL, NZL), F32)
    pair = pltpu.VMEM((2, NXL, NZL), F32)
    tile = pltpu.VMEM((8, NZL), F32)
    tiles = pltpu.VMEM((3, 8, NZL), F32)
    dma = pltpu.SemaphoreType.DMA
    in_hbm = pl.BlockSpec(memory_space=pltpu.HBM)
    in_vmem = pl.BlockSpec(memory_space=pltpu.VMEM)
    out_shape = (
        jax.ShapeDtypeStruct((3, NXL, NYL, NZL), F32),
        jax.ShapeDtypeStruct((NXL, NYL, NZL), F32),
    )
    inputs = [
        pltpu.with_memory_space_constraint(a, pltpu.HBM) for a in (phase_mask, pressure, velocity_cot)
    ]
    outs = pl.pallas_call(
        body,
        out_shape=out_shape,
        in_specs=[in_hbm] * 3,
        out_specs=(in_vmem, in_vmem),
        scratch_shapes=[
            pltpu.VMEM((NXL, NYL, NZL), jnp.int32),
            *[field] * 8,
            pltpu.VMEM((NXL + 1, NYL, NZL), F32),
            *[block] * 4,
            pair,
            *[block] * 4,
            pltpu.VMEM((3, 3, NXL, NYL, NZL), F32),
            pltpu.VMEM((4, NXL, NYL, NZL), F32),
            *[pltpu.VMEM((2, 2 * NYL + 8, NZL), F32)] * 2,
            *[pltpu.VMEM((2, 2 * NXL + 8, NZL), F32)] * 2,
            *[tiles] * 3,
            *[pltpu.VMEM((2, NYL, NZL), F32)] * 2,
            *[pair] * 2,
            *[tile] * 3,
            pltpu.VMEM((4, NXL, NZL), F32),
            pltpu.VMEM((4, 8, NZL), F32),
            pltpu.VMEM((4, 8, NZL), F32),
            pltpu.VMEM((4, NXL, NZL), F32),
            *[flat] * 3,
            pltpu.VMEM((2, NYL, NZL), F32), pltpu.VMEM((NYL, NZL), F32), pair, flat,
            *[flat] * 4,
            *[flats] * 2,
            pltpu.VMEM((3, 2, NXL, NZL), F32),
            pltpu.VMEM((3, 2, NYL, NZL), F32),
            *[tile] * 8,
            pltpu.VMEM((2, 8, NZL), F32),
            *[tiles] * 4,
            pltpu.VMEM((sum(RING ** len(axes) for axes in PHASES), 1, NZL), F32),
            dma((5,)),
            dma((15,)), dma((15,)), dma((3, 6)), dma((3, 6)),
            dma((len(PHASES),)), dma((len(PHASES),)),
            pltpu.SemaphoreType.REGULAR,
            pltpu.SemaphoreType.REGULAR((3, 3)),
            dma((28,)), dma((28,)),
        ],
        compiler_params=pltpu.CompilerParams(
            collective_id=0, has_side_effects=True, vmem_limit_bytes=24 * 1024 * 1024
        ),
        name="projection_adjoint",
    )(*inputs)
    return pl.pallas_call(
        save,
        out_shape=out_shape,
        in_specs=[in_vmem] * 2,
        out_specs=(in_hbm, in_hbm),
        scratch_shapes=[dma((2,))],
        compiler_params=pltpu.CompilerParams(vmem_limit_bytes=4 * 1024 * 1024),
        name="save",
    )(*outs)


def solution(mesh):
    in_specs = (P("gx", "gy", "gz"), P("gx", "gy", "gz"), P(None, "gx", "gy", "gz"))
    out_specs = (P(None, "gx", "gy", "gz"), P("gx", "gy", "gz"))
    return jax.shard_map(
        on_device, mesh=mesh, in_specs=in_specs, out_specs=out_specs, check_vma=False
    )
```

```python
import jax
import jax.numpy as jnp
from jax import lax
from jax.experimental import pallas as pl
from jax.experimental.pallas import tpu as pltpu
from jax.sharding import PartitionSpec as P


MESH = pl.DeviceIdType.MESH
AXES = ("gx", "gy", "gz")
RING = 8
NXL, NYL, NZL = 16, 32, 128
TOP = 8
LAST = TOP + NYL - 1
BLOCKS = NYL // 8
F32 = jnp.float32
PHASES = (("gy",), ("gx", "gz"))


def two_sum(a, b):
    s = a + b
    t = s - a
    return s, (a - (s - t)) + (b - t)


def split(a):
    c = 4097.0 * a
    hi = c - (c - a)
    return hi, a - hi


def sub_mul(x, c, y):
    p = c * y[0]
    ch, cl = split(c)
    yh, yl = split(y[0])
    err = ((ch * yh - p) + ch * yl + cl * yh) + cl * yl
    s, t = two_sum(x[0], -p)
    t = t + (x[1] - (err + c * y[1]))
    hi = s + t
    return hi, t - (hi - s)


def galerkin(sums):
    g0, g2, h00, h01, h02, h11, h12, h22 = sums
    one = jnp.ones_like(g0[0])
    g1 = sub_mul(h00, one, g0)
    a = h01[0] / h00[0]
    b = h02[0] / h00[0]
    h01p = sub_mul(h01, a, h00)
    h02p = sub_mul(h02, b, h00)
    h11p = sub_mul(sub_mul(h11, a, h01), a, h01p)
    h12p = sub_mul(sub_mul(h12, a, h02), b, h01p)
    h22p = sub_mul(sub_mul(h22, b, h02), b, h02p)
    g1p = sub_mul(g1, a, g0)
    g2p = sub_mul(g2, b, g0)
    ok1 = h11p[0] > 1e-10 * h11[0]
    inv1 = jnp.where(ok1, 1.0 / jnp.where(ok1, h11p[0], 1.0), 0.0)
    c = h12p[0] * inv1
    h12q = sub_mul(h12p, c, h11p)
    h22q = sub_mul(sub_mul(h22p, c, h12p), c, h12q)
    g2q = sub_mul(g2p, c, g1p)
    h02q = h02p[0] - c * h01p[0]
    ok2 = h22q[0] > 1e-10 * h22[0]
    y2 = jnp.where(ok2, g2q[0] / jnp.where(ok2, h22q[0], 1.0), 0.0)
    y1p = (g1p[0] - h12q[0] * y2) * inv1
    y0p = (g0[0] - h01p[0] * y1p - h02q * y2) / h00[0]
    return y0p - a * y1p - (b - c * a) * y2, y1p - c * y2, y2


def roll(x, shift, axis):
    return pltpu.roll(x, shift, axis)


def remote(src, dst, send, recv, device):
    return pltpu.make_async_remote_copy(
        src_ref=src, dst_ref=dst, send_sem=send, recv_sem=recv, device_id=device, device_id_type=MESH
    )


def body(
    mask_hbm, press_hbm, vel_hbm, out_u, out_c,
    mask, fc, fp, fu0, fu1, fu2, fv0, fv1, fv2,
    wx, wyu, wyd, wzu, wzd, wyb, minv, rhs, img, part,
    grads, bases,
    kx_out, kx_in, ky_out, ky_in, kz_out, kz_lo, kz_hi,
    tx_out, tx_in, ty_out, ty_in, tz_out, tz_lo, tz_hi,
    dxy, dxz, dyz, dyz_rows,
    cyup, cydn, uyup, cx_in, ux_in, cy_in, uy_in, pyup, pydn, pyup_in, pydn_in, vyup, vydn, vy_in, vx_in,
    cz, cz_lo, cz_hi, uz, uz_lo, pz, pz_lo, pz_hi, zmix, vz, vz_lo, vz_hi, vmix,
    sums,
    load_sem,
    send1, recv1, sendv, recvv, sendr, recvr, ready, token, sendk, recvk,
):
    pos = {axis: lax.axis_index(axis) for axis in AXES}
    fwd = {axis: lax.rem(pos[axis] + 1, RING) for axis in AXES}
    bwd = {axis: lax.rem(pos[axis] + RING - 1, RING) for axis in AXES}
    lane = lax.broadcasted_iota(jnp.int32, (8, NZL), 1)
    sub = lax.broadcasted_iota(jnp.int32, (8, NZL), 0)
    half = lane // 2
    even = lane - 2 * half == 0
    first = lane == 0
    final = lane == NZL - 1
    border = jnp.logical_or(first, final)

    low = {axis: pos[axis] == 0 for axis in AXES}
    high = {axis: pos[axis] == RING - 1 for axis in AXES}

    class Shift:
        def __init__(self, src, dst, send, recv, *moves):
            moves = tuple(zip(moves[::2], moves[1::2]))
            device = {axis: fwd[axis] if up else bwd[axis] for axis, up in moves}
            self.copy = remote(src, dst, send, recv, device)
            self.sends = self.receives = None
            for axis, up in moves:
                sends = jnp.logical_not(high[axis] if up else low[axis])
                receives = jnp.logical_not(low[axis] if up else high[axis])
                self.sends = sends if self.sends is None else jnp.logical_and(self.sends, sends)
                self.receives = receives if self.receives is None else jnp.logical_and(self.receives, receives)

        def start(self):
            pl.when(self.sends)(lambda: self.copy.start())

        def wait_recv(self):
            pl.when(self.receives)(lambda: self.copy.wait_recv())

        def wait_send(self):
            pl.when(self.sends)(lambda: self.copy.wait_send())

    def tell(stage):
        for a, axis in enumerate(AXES):
            for end, other in ((high[axis], fwd[axis]), (low[axis], bwd[axis])):

                @pl.when(end)
                def _(a=a, axis=axis, other=other):
                    pl.semaphore_signal(
                        token.at[stage, a], inc=1, device_id={axis: other}, device_id_type=MESH
                    )

    def heard(stage):
        for a, axis in enumerate(AXES):

            @pl.when(jnp.logical_or(high[axis], low[axis]))
            def _(a=a):
                pl.semaphore_wait(token.at[stage, a], 1)

    cells = (pl.ds(1, NXL), pl.ds(TOP, NYL))
    loads = [pltpu.make_async_copy(mask_hbm, mask, load_sem.at[0])]
    for i, field in ((2, fu2), (1, fu1), (0, fu0)):
        loads.append(pltpu.make_async_copy(vel_hbm.at[i], field.at[cells], load_sem.at[1 + i]))
    loads.append(pltpu.make_async_copy(press_hbm, fp.at[cells], load_sem.at[4]))
    for load in loads:
        load.start()

    inner = pl.ds(TOP, NYL)
    plane = jnp.zeros((NYL, NZL), F32)
    line = jnp.zeros((1, NZL), F32)
    zero = jnp.zeros((8, NZL), F32)
    for buffer in (ux_in, cy_in, uy_in, cz_lo, cz_hi, uz_lo):
        buffer[...] = jnp.zeros(buffer.shape, F32)
    cx_in[...] = jnp.full(cx_in.shape, 3, jnp.int32)

    barrier = pltpu.get_barrier_semaphore()
    for axis in AXES:
        for other in (fwd[axis], bwd[axis]):
            pl.semaphore_signal(barrier, inc=1, device_id={axis: other}, device_id_type=MESH)
    for field in (fc, fp, fu0, fv0, fv1, fv2):
        field[0, inner] = plane
        field[NXL + 1, inner] = plane
    for x in range(1, NXL + 1):
        fu1[x, pl.ds(TOP - 1, 1)] = line
        for field in (fc, fv0, fv1, fv2):
            field[x, pl.ds(TOP - 1, 1)] = line
            field[x, pl.ds(LAST + 1, 1)] = line
    for buffer in (
        pyup_in, pydn_in, vy_in, vx_in,
        pz_lo, pz_hi, vz_lo, vz_hi,
        kx_in, ky_in, kz_lo, kz_hi, tx_in, ty_in, tz_lo, tz_hi, dxy, dxz, dyz, dyz_rows, kx_out, ky_out,
    ):
        buffer[...] = jnp.zeros(buffer.shape, F32)

    def pick(x, k, value, packed):
        return jnp.where(half == BLOCKS * x + k, roll(value, 2 * BLOCKS * x + 2 * k + 1, 1), packed)

    def place(x, k, mixed):
        return roll(mixed, NZL - 1 - 2 * BLOCKS * x - 2 * k, 1)

    def above(value, edge):
        return jnp.where(final, edge, roll(value, NZL - 1, 1))

    def below(value, edge):
        return jnp.where(first, edge, roll(value, 1, 1))

    pl.semaphore_wait(barrier, 6)
    sent = []

    def launch(copies):
        for copy in copies:
            copy.start()
        sent.extend(copies)
        return copies

    round1 = launch([
        Shift(mask_hbm.at[NXL - 1], cx_in.at[0], send1.at[0], recv1.at[0], "gx", True),
        Shift(mask_hbm.at[0], cx_in.at[1], send1.at[1], recv1.at[1], "gx", False),
        Shift(vel_hbm.at[0, NXL - 1], ux_in, send1.at[7], recv1.at[7], "gx", True),
    ])
    loads[0].wait()

    def coefficient(phase):
        c = jnp.where(phase == 0, 8.0, jnp.where(phase == 1, 1.0, jnp.where(phase == 2, 2.0, 0.0)))
        return c.astype(F32)

    def prepare(x, packed):
        for k in range(BLOCKS):
            c = coefficient(mask[x, pl.ds(8 * k, 8)])
            fc[x + 1, pl.ds(TOP + 8 * k, 8)] = c
            packed = pick(x, k, c, packed)
            if k == 0:
                cydn[pl.ds(x, 1)] = c[0:1]
            if k == BLOCKS - 1:
                cyup[pl.ds(x, 1)] = c[7:8]
        return packed

    cz[...] = lax.fori_loop(0, NXL, prepare, zero, unroll=4)
    round1 += launch([
        Shift(cz, cz_lo, send1.at[4], recv1.at[4], "gz", True),
        Shift(cz, cz_hi, send1.at[5], recv1.at[5], "gz", False),
        Shift(cyup, cy_in.at[0], send1.at[2], recv1.at[2], "gy", True),
        Shift(cydn, cy_in.at[1], send1.at[3], recv1.at[3], "gy", False),
    ])
    for load in loads[1:4]:
        load.wait()

    def velocity(x, packed):
        for k in range(BLOCKS):
            packed = pick(x, k, fu2[x + 1, pl.ds(TOP + 8 * k, 8)], packed)
        uyup[pl.ds(x, 1)] = fu1[x + 1, pl.ds(LAST, 1)]
        return packed

    uz[...] = lax.fori_loop(0, NXL, velocity, zero, unroll=4)
    round1 += launch([
        Shift(uz, uz_lo, send1.at[6], recv1.at[6], "gz", True),
        Shift(uyup, uy_in, send1.at[8], recv1.at[8], "gy", True),
    ])
    tell(0)
    loads[4].wait()

    def mix(lo, hi):
        return jnp.where(even, roll(hi, NZL - 1, 1), roll(lo, 1, 1))

    def weigh(x, carry):
        pw, pp = carry
        for k in range(BLOCKS):
            r = TOP + 8 * k
            rows, own = pl.ds(r, 8), pl.ds(8 * k, 8)
            c = fc[x + 1, rows]
            xu = 0.5 * (c + fc[x + 2, rows])
            xd = 0.5 * (c + fc[x, rows])
            yu = 0.5 * (c + fc[x + 1, pl.ds(r + 1, 8)])
            yd = 0.5 * (c + fc[x + 1, pl.ds(r - 1, 8)])
            zu = 0.5 * (c + above(c, 0.0))
            zd = 0.5 * (c + below(c, 0.0))
            u2 = fu2[x + 1, rows]
            wx[x + 1, own] = xu
            wyu[x, own] = yu
            wyd[x, own] = yd
            wzu[x, own] = zu
            wzd[x, own] = zd
            minv[x, own] = (xd + xu) + (yd + yu) + (zd + zu)
            rhs[x, own] = (
                (xu * fu0[x + 1, rows] - xd * fu0[x, rows])
                + (yu * fu1[x + 1, rows] - yd * fu1[x + 1, pl.ds(r - 1, 8)])
                + (zu * u2 - zd * below(u2, 0.0))
            )
            pw = pick(x, k, jnp.where(first, zd, zu), pw)
            p = fp[x + 1, rows]
            pp = pick(x, k, p, pp)
            if k == 0:
                pydn[pl.ds(x, 1)] = p[0:1]
            if k == BLOCKS - 1:
                pyup[pl.ds(x, 1)] = p[7:8]
        return pw, pp

    pw, pp = lax.fori_loop(0, NXL, weigh, (zero, zero), unroll=4)
    pz[...] = pp
    later = [
        Shift(fp.at[NXL, inner], fp.at[0, inner], send1.at[9], recv1.at[9], "gx", True),
        Shift(fp.at[1, inner], fp.at[NXL + 1, inner], send1.at[10], recv1.at[10], "gx", False),
        Shift(pyup, pyup_in, send1.at[11], recv1.at[11], "gy", True),
        Shift(pydn, pydn_in, send1.at[12], recv1.at[12], "gy", False),
        Shift(pz, pz_lo, send1.at[13], recv1.at[13], "gz", True),
        Shift(pz, pz_hi, send1.at[14], recv1.at[14], "gz", False),
    ]
    for copy in round1:
        copy.wait_recv()

    h = 0.5 * coefficient(cx_in[0])
    w = 0.5 * fc[1, inner] + h
    wx[0] = w
    minv[0] = minv[0] + h
    rhs[0] = rhs[0] - w * ux_in[...]
    h = 0.5 * coefficient(cx_in[1])
    wx[NXL] = wx[NXL] + h
    minv[NXL - 1] = minv[NXL - 1] + h
    rhs[NXL - 1] = rhs[NXL - 1] + h * fu0[NXL, inner]
    for x in range(NXL):
        row, top, bottom = pl.ds(x, 1), pl.ds(0, 1), pl.ds(NYL - 1, 1)
        h = 0.5 * cy_in[0, row]
        w = wyd[x, top] + h
        wyd[x, top] = w
        wyb[0, row] = w
        minv[x, top] = minv[x, top] + h
        rhs[x, top] = rhs[x, top] - w * uy_in[row]
        h = 0.5 * cy_in[1, row]
        w = wyu[x, bottom] + h
        wyu[x, bottom] = w
        wyb[1, row] = w
        minv[x, bottom] = minv[x, bottom] + h
        rhs[x, bottom] = rhs[x, bottom] + h * uyup[row]
    hz = 0.5 * mix(cz_lo[...], cz_hi[...])
    pw = pw + hz
    uz_mix = roll(uz_lo[...], 1, 1)
    zmix[1] = uz_mix
    pr = jnp.where(even, hz * uz[...], -pw * uz_mix)

    def faces(i, x, k, value):
        if k == 0:
            vydn[i, pl.ds(x, 1)] = value[0:1]
        if k == BLOCKS - 1:
            vyup[i, pl.ds(x, 1)] = value[7:8]

    def start(x, carry):
        packed, g0 = carry
        for k in range(BLOCKS):
            own = pl.ds(8 * k, 8)
            m = 1.0 / (minv[x, own] + jnp.where(border, place(x, k, hz), 0.0))
            r0 = rhs[x, own] + jnp.where(border, place(x, k, pr), 0.0)
            v = m * r0
            minv[x, own] = m
            rhs[x, own] = r0
            fv0[x + 1, pl.ds(TOP + 8 * k, 8)] = v
            packed = pick(x, k, v, packed)
            faces(0, x, k, v)
            g0 = g0 + v * r0
        return packed, g0

    packed, g0 = lax.fori_loop(0, NXL, start, (zero,) * 2, unroll=4)

    def exchange(i, field, packed):
        vz[i] = packed
        copies = [
            Shift(field.at[NXL, inner], vx_in.at[i, 0], sendv.at[i, 0], recvv.at[i, 0], "gx", True),
            Shift(field.at[1, inner], vx_in.at[i, 1], sendv.at[i, 1], recvv.at[i, 1], "gx", False),
            Shift(vyup.at[i], vy_in.at[i, 0], sendv.at[i, 2], recvv.at[i, 2], "gy", True),
            Shift(vydn.at[i], vy_in.at[i, 1], sendv.at[i, 3], recvv.at[i, 3], "gy", False),
            Shift(vz.at[i], vz_lo.at[i], sendv.at[i, 4], recvv.at[i, 4], "gz", True),
            Shift(vz.at[i], vz_hi.at[i], sendv.at[i, 5], recvv.at[i, 5], "gz", False),
        ]
        launch(copies)
        if i == 0:
            launch(later)
        heard(i)
        tell(i + 1)
        return copies

    def interior(i, field):
        def plane_of(x, carry):
            dot, packed = carry
            for k in range(BLOCKS):
                r = TOP + 8 * k
                rows, own = pl.ds(r, 8), pl.ds(8 * k, 8)
                v = field[x + 1, rows]
                q = (
                    (wx[x, own] * (v - field[x, rows]) + wx[x + 1, own] * (v - field[x + 2, rows]))
                    + (
                        wyd[x, own] * (v - field[x + 1, pl.ds(r - 1, 8)])
                        + wyu[x, own] * (v - field[x + 1, pl.ds(r + 1, 8)])
                    )
                    + (wzd[x, own] * (v - below(v, 0.0)) + wzu[x, own] * (v - above(v, 0.0)))
                )
                part[x, own] = q
                if i == 1:
                    packed = pick(x, k, q, packed)
                if i == 2:
                    dot = dot + v * q
            return dot, packed

        return lax.fori_loop(0, NXL, plane_of, (zero, zero), unroll=4)

    def arrive(i, copies):
        for copy in copies:
            copy.wait_recv()
        vmix[i] = mix(vz_lo[i], vz_hi[i])
        return pw * vmix[i] - hz * vz[i]

    def join(i):
        part[0] = part[0] - wx[0] * vx_in[i, 0]
        part[NXL - 1] = part[NXL - 1] - wx[NXL] * vx_in[i, 1]
        for x in range(NXL):
            row = pl.ds(x, 1)
            part[x, 0:1] = part[x, 0:1] - wyb[0, row] * vy_in[i, 0, row]
            part[x, NYL - 1 : NYL] = part[x, NYL - 1 : NYL] - wyb[1, row] * vy_in[i, 1, row]

    def around(x, k, i, field):
        r = TOP + 8 * k
        rows = pl.ds(r, 8)
        v = field[x + 1, rows]
        edge = place(x, k, vmix[i])
        return (
            v,
            (field[x + 2, rows], field[x + 1, pl.ds(r + 1, 8)], above(v, edge)),
            (field[x, rows], field[x + 1, pl.ds(r - 1, 8)], below(v, edge)),
        )

    copies = exchange(0, fv0, packed)
    interior(0, fv0)

    def at_border(x, k, mixed):
        return jnp.where(border, place(x, k, mixed), 0.0)

    def spread_rows(x, carry):
        pm, py = carry
        row = pl.ds(x, 1)
        for k in range(BLOCKS):
            own = pl.ds(8 * k, 8)
            m = minv[x, own]
            pm = pick(x, k, m, pm)
            if k == 0:
                py = pick(x, k, jnp.where(sub == 0, wyd[x, own], 0.0), py)
                ky_out[0, row] = m[0:1] * wyb[0, row]
                ky_out[0, pl.ds(NXL + x, 1)] = (m * at_border(x, k, pw))[0:1]
            if k == BLOCKS - 1:
                py = pick(x, k, jnp.where(sub == 7, wyu[x, own], 0.0), py)
                ky_out[1, row] = m[7:8] * wyb[1, row]
                ky_out[1, pl.ds(NXL + x, 1)] = (m * at_border(x, k, pw))[7:8]
        return pm, py

    pm, py = lax.fori_loop(0, NXL, spread_rows, (zero, zero))
    px = zero
    for side, p, wp in ((0, 0, 0), (1, NXL - 1, NXL)):
        for k in range(BLOCKS):
            own = pl.ds(8 * k, 8)
            px = pick(p, k, wx[wp, own], px)
            kx_out[side, own] = minv[p, own] * wx[wp, own]
            kx_out[side, pl.ds(NYL + 8 * k, 8)] = minv[p, own] * at_border(p, k, pw)
        for end, y in ((0, 0), (1, NYL - 1)):
            m = minv[p, pl.ds(y, 1)]
            kx_out[side, pl.ds(2 * NYL + end, 1)] = m * wyb[end, pl.ds(p, 1)]
            ky_out[end, pl.ds(2 * NXL + side, 1)] = m * wx[wp, pl.ds(y, 1)]
    kz_out[0] = pm * pw
    kz_out[1] = pm * px
    kz_out[2] = pm * py
    statics = launch([
        Shift(kx_out.at[1], kx_in.at[0], sendk.at[0], recvk.at[0], "gx", True),
        Shift(kx_out.at[0], kx_in.at[1], sendk.at[1], recvk.at[1], "gx", False),
        Shift(ky_out.at[1], ky_in.at[0], sendk.at[2], recvk.at[2], "gy", True),
        Shift(ky_out.at[0], ky_in.at[1], sendk.at[3], recvk.at[3], "gy", False),
        Shift(kz_out, kz_lo, sendk.at[4], recvk.at[4], "gz", True),
        Shift(kz_out, kz_hi, sendk.at[5], recvk.at[5], "gz", False),
    ])
    pq = arrive(0, copies)
    join(0)

    def step0(x, carry):
        packed, h00, h01 = carry
        for k in range(BLOCKS):
            own, rows = pl.ds(8 * k, 8), pl.ds(TOP + 8 * k, 8)
            v = fv0[x + 1, rows]
            q = part[x, own] - jnp.where(border, place(x, k, pq), 0.0)
            w = minv[x, own] * q - v
            img[x, own] = q
            fv1[x + 1, rows] = w
            packed = pick(x, k, w, packed)
            faces(1, x, k, w)
            h00 = h00 + v * q
            h01 = h01 + w * q
        return packed, h00, h01

    packed, h00, h01 = lax.fori_loop(0, NXL, step0, (zero, zero, zero), unroll=4)
    copies = exchange(1, fv1, packed)
    diagonal = []
    n = 12
    for a, up_a in enumerate((True, False)):
        for b, up_b in enumerate((True, False)):
            slot = 2 * a + b
            rows_b = (vyup if up_b else vydn).at[1]
            rows_a = (vyup if up_a else vydn).at[1]
            for src, dst, moves in (
                (rows_b, dxy, ("gx", up_a, "gy", up_b)),
                (vz.at[1], dxz, ("gx", up_a, "gz", up_b)),
                (vz.at[1], dyz, ("gy", up_a, "gz", up_b)),
                (rows_a, dyz_rows, ("gy", up_a, "gz", up_b)),
            ):
                diagonal.append(Shift(src, dst.at[slot], sendk.at[n], recvk.at[n], *moves))
                n += 1
    launch(diagonal)
    _, packed_part = interior(1, fv1)
    hv = hz * vz[1]
    tz_out[...] = pm * (packed_part + hv) - vz[1]
    for side, p in ((0, 0), (1, NXL - 1)):
        for k in range(BLOCKS):
            own = pl.ds(8 * k, 8)
            tx_out[side, own] = (
                minv[p, own] * (part[p, own] + at_border(p, k, hv)) - fv1[p + 1, pl.ds(TOP + 8 * k, 8)]
            )
    for x in range(NXL):
        row = pl.ds(x, 1)
        for side, k, y, r in ((0, 0, 0, 0), (1, BLOCKS - 1, NYL - 1, 7)):
            own = (vydn if side == 0 else vyup)[1, row]
            at = pl.ds(y, 1)
            ty_out[side, row] = minv[x, at] * (part[x, at] + at_border(x, k, hv)[r : r + 1]) - own
    partial = launch([
        Shift(tx_out.at[1], tx_in.at[0], sendk.at[6], recvk.at[6], "gx", True),
        Shift(tx_out.at[0], tx_in.at[1], sendk.at[7], recvk.at[7], "gx", False),
        Shift(ty_out.at[1], ty_in.at[0], sendk.at[8], recvk.at[8], "gy", True),
        Shift(ty_out.at[0], ty_in.at[1], sendk.at[9], recvk.at[9], "gy", False),
        Shift(tz_out, tz_lo, sendk.at[10], recvk.at[10], "gz", True),
        Shift(tz_out, tz_hi, sendk.at[11], recvk.at[11], "gz", False),
    ])
    pq = arrive(1, copies)
    join(1)

    def step1(x, carry):
        packed, h11, h12, h02, g2 = carry
        for k in range(BLOCKS):
            own, rows = pl.ds(8 * k, 8), pl.ds(TOP + 8 * k, 8)
            v = fv1[x + 1, rows]
            q = part[x, own] - jnp.where(border, place(x, k, pq), 0.0)
            w = minv[x, own] * q - v
            fv2[x + 1, rows] = w
            packed = pick(x, k, w, packed)
            faces(2, x, k, w)
            h11 = h11 + v * q
            h12 = h12 + w * q
            h02 = h02 + w * img[x, own]
            g2 = g2 + w * rhs[x, own]
        return packed, h11, h12, h02, g2

    packed, h11, h12, h02, g2 = lax.fori_loop(0, NXL, step1, (zero,) * 5, unroll=4)
    inside, _ = interior(2, fv2)
    heard(2)
    for d in range(1, RING):
        pl.semaphore_signal(
            ready, inc=1, device_id={"gz": lax.rem(pos["gz"] + d, RING)}, device_id_type=MESH
        )
    for copy in statics + partial + diagonal:
        copy.wait_recv()
    mixed_x = [mix(dxz[2 * side], dxz[2 * side + 1]) for side in (0, 1)]
    mixed_y = [mix(dyz[2 * side], dyz[2 * side + 1]) for side in (0, 1)]
    for side, p, mine in ((0, NXL - 1, 1), (1, 0, NXL)):
        for k in range(BLOCKS):
            own = pl.ds(8 * k, 8)
            vx_in[2, side, own] = (
                tx_in[side, own]
                - kx_in[side, own] * fv1[mine, pl.ds(TOP + 8 * k, 8)]
                - kx_in[side, pl.ds(NYL + 8 * k, 8)] * place(p, k, mixed_x[side])
            )
        for end, y in ((0, 0), (1, NYL - 1)):
            at = pl.ds(y, 1)
            vx_in[2, side, at] = vx_in[2, side, at] - (
                kx_in[side, pl.ds(2 * NYL + end, 1)] * dxy[2 * side + end, pl.ds(p, 1)]
            )
    for side in (0, 1):
        own_rows = vydn if side == 0 else vyup
        for block in range(NXL // 8):
            xs = pl.ds(8 * block, 8)
            beside = jnp.where(
                first, roll(dyz_rows[2 * side, xs], 1, 1), roll(dyz_rows[2 * side + 1, xs], NZL - 1, 1)
            )
            vy_in[2, side, xs] = (
                ty_in[side, xs]
                - ky_in[side, xs] * own_rows[1, xs]
                - ky_in[side, pl.ds(NXL + 8 * block, 8)] * beside
            )
        for end, x, far in ((0, 0, NXL - 1), (1, NXL - 1, 0)):
            at = pl.ds(x, 1)
            vy_in[2, side, at] = vy_in[2, side, at] - (
                ky_in[side, pl.ds(2 * NXL + end, 1)] * dxy[2 * end + side, pl.ds(far, 1)]
            )
    beside_x = jnp.where(lane < 64, roll(mixed_x[0], 2 * BLOCKS, 1), roll(mixed_x[1], NZL - 2 * BLOCKS, 1))
    step_k = 2 * (BLOCKS - 1)
    beside_y = jnp.where(
        sub == 0,
        roll(roll(mixed_y[0], NZL - step_k, 1), 1, 0),
        roll(roll(mixed_y[1], step_k, 1), 7, 0),
    )
    kz = [mix(kz_lo[i], kz_hi[i]) for i in range(3)]
    vmix[2] = (
        mix(tz_lo[...], tz_hi[...]) - kz[0] * vz[1] - kz[1] * beside_x - kz[2] * beside_y
    )
    pq = pw * vmix[2] - hz * packed
    outside = packed * pq
    for k in range(BLOCKS):
        own, rows = pl.ds(8 * k, 8), pl.ds(TOP + 8 * k, 8)
        outside = outside + (
            wx[0, own] * fv2[1, rows] * vx_in[2, 0, own] + wx[NXL, own] * fv2[NXL, rows] * vx_in[2, 1, own]
        )
    for half_x in range(NXL // 8):
        xs = pl.ds(8 * half_x, 8)
        outside = outside + (
            wyb[0, xs] * vydn[2, xs] * vy_in[2, 0, xs] + wyb[1, xs] * vyup[2, xs] * vy_in[2, 1, xs]
        )
    h22 = inside - outside

    level = [(value, None) for value in (g0, g2, h00, h01, h02, h11, h12, h22)]
    for width in (4, 2, 1):
        keep = lax.rem(sub // width, 2) == 0
        merged = []
        n = len(level) // 2
        for i in range(n):
            (ah, al), (bh, bl) = level[i], level[i + n]
            hi, err = two_sum(jnp.where(keep, ah, bh), roll_rows(jnp.where(keep, bh, ah), width, keep))
            if al is not None:
                err = err + (jnp.where(keep, al, bl) + roll_rows(jnp.where(keep, bl, al), width, keep))
            merged.append((hi, err))
        level = merged
    hi, lo = level[0]
    for width in (64, 32, 16, 8, 4, 2, 1):
        hi, err = two_sum(hi, roll(hi, width, 1))
        lo = (lo + roll(lo, width, 1)) + err
    own_row = jnp.where(lane == sub, hi, 0.0) + jnp.where(lane == sub + 64, lo, 0.0)
    row = jnp.sum(own_row, axis=0, keepdims=True)

    low_half = lax.broadcasted_iota(jnp.int32, (1, NZL), 1) < 64

    slot0 = 0
    drains = []
    for phase, axes in enumerate(PHASES):
        count = RING ** len(axes)
        mine = 0
        for axis in axes:
            mine = mine * RING + pos[axis]
        slots = sums.at[pl.ds(slot0, count)]
        slots[mine] = row
        if len(axes) > 1:
            pl.semaphore_wait(ready, RING - 1)
        offsets = [()]
        for axis in axes:
            offsets = [o + (d,) for o in offsets for d in range(RING)]
        offsets = sorted(offsets[1:], key=lambda o: urgency(o))
        for o in offsets:
            device = {axis: lax.rem(pos[axis] + d, RING) for axis, d in zip(axes, o) if d}
            remote(slots.at[mine], slots.at[mine], sendr.at[phase], recvr.at[phase], device).start()
        if phase == 0:
            for copy in later:
                copy.wait_recv()
            zmix[0] = mix(pz_lo[...], pz_hi[...])
            fu0[0, inner] = ux_in[...]
            for i, field in enumerate((fv0, fv1, fv2)):
                field[0, inner] = vx_in[i, 0]
                field[NXL + 1, inner] = vx_in[i, 1]
            for x in range(NXL):
                lrow = pl.ds(x, 1)
                fu1[x + 1, pl.ds(TOP - 1, 1)] = uy_in[lrow]
                fp[x + 1, pl.ds(TOP - 1, 1)] = pyup_in[lrow]
                fp[x + 1, pl.ds(LAST + 1, 1)] = pydn_in[lrow]
                for i, field in enumerate((fv0, fv1, fv2)):
                    field[x + 1, pl.ds(TOP - 1, 1)] = vy_in[i, 0, lrow]
                    field[x + 1, pl.ds(LAST + 1, 1)] = vy_in[i, 1, lrow]

            def terms(x, carry):
                for k in range(BLOCKS):
                    r = TOP + 8 * k
                    rows, own = pl.ds(r, 8), pl.ds(8 * k, 8)
                    p = fp[x + 1, rows]
                    pe = place(x, k, zmix[0])
                    gu = (
                        -0.5 * (fp[x + 2, rows] - p),
                        -0.5 * (fp[x + 1, pl.ds(r + 1, 8)] - p),
                        -0.5 * (above(p, pe) - p),
                    )
                    gd = (
                        -0.5 * (p - fp[x, rows]),
                        -0.5 * (p - fp[x + 1, pl.ds(r - 1, 8)]),
                        -0.5 * (p - below(p, pe)),
                    )
                    u2 = fu2[x + 1, rows]
                    bases[0, x, own] = (
                        (gd[0] * fu0[x, rows] + gu[0] * fu0[x + 1, rows])
                        + (gd[1] * fu1[x + 1, pl.ds(r - 1, 8)] + gu[1] * fu1[x + 1, rows])
                        + (gd[2] * below(u2, place(x, k, zmix[1])) + gu[2] * u2)
                    )
                    for i, field in enumerate((fv0, fv1, fv2)):
                        v, up, down = around(x, k, i, field)
                        total = None
                        for dim in range(3):
                            upper, lower = up[dim] - v, v - down[dim]
                            grads[i, dim, x, own] = upper
                            term = gd[dim] * lower + gu[dim] * upper
                            total = term if total is None else total + term
                        bases[1 + i, x, own] = total
                return carry

            lax.fori_loop(0, NXL, terms, 0)
        others = sums.at[pl.ds(slot0, count - 1)]
        pltpu.make_async_copy(others, others, recvr.at[phase]).wait()
        drains.append(pltpu.make_async_copy(others, others, sendr.at[phase]))
        parts = [sums[slot0 + i] for i in range(count)]
        errs = []
        while len(parts) > 1:
            pairs = [two_sum(parts[i], parts[i + 1]) for i in range(0, len(parts), 2)]
            parts = [s for s, _ in pairs]
            errs.append(sum_tree([e for _, e in pairs]))
        total, err = parts[0], sum_tree(errs)
        row = jnp.where(low_half, total, total + roll(err, 64, 1))
        slot0 += count

    spread = jnp.broadcast_to(row, (8, NZL))
    col_hi = jnp.sum(jnp.where(lane == sub, spread, 0.0), axis=1, keepdims=True)
    col_lo = jnp.sum(jnp.where(lane == sub + 64, spread, 0.0), axis=1, keepdims=True)
    col_hi = jnp.broadcast_to(col_hi, (8, NZL))
    col_lo = jnp.broadcast_to(col_lo, (8, NZL))
    order = ROW_OF
    sums_hi_lo = [(col_hi[order[i] : order[i] + 1], col_lo[order[i] : order[i] + 1]) for i in range(8)]
    y = [jnp.broadcast_to(value, (8, NZL)) for value in galerkin(sums_hi_lo)]

    def finish(x, carry):
        for k in range(BLOCKS):
            rows, own = pl.ds(TOP + 8 * k, 8), pl.ds(8 * k, 8)
            for dim, field in enumerate((fu0, fu1, fu2)):
                grad = y[0] * grads[0, dim, x, own] + y[1] * grads[1, dim, x, own] + y[2] * grads[2, dim, x, own]
                out_u[dim, x, own] = field[x + 1, rows] + grad
            out_c[x, own] = bases[0, x, own] + (
                y[0] * bases[1, x, own] + y[1] * bases[2, x, own] + y[2] * bases[3, x, own]
            )
        return carry

    lax.fori_loop(0, NXL, finish, 0, unroll=4)
    for drain in drains:
        drain.wait()
    for copy in sent:
        copy.wait_send()


def roll_rows(x, width, keep):
    if width == 4:
        return roll(x, 4, 0)
    return jnp.where(keep, roll(x, 8 - width, 0), roll(x, width, 0))


def urgency(offset):
    steps = [min(d, RING - d) for d in offset]
    if len(offset) == 1:
        return -steps[0]
    return (offset[0] + RING - 1) % RING + (RING // 2 - steps[1]) - 0.75 * sum(steps)


def sum_tree(values):
    total = values[0]
    for value in values[1:]:
        total = total + value
    return total


def row_order():
    level = [{i: set(range(8))} for i in range(8)]
    names = [[i] * 8 for i in range(8)]
    for width in (4, 2, 1):
        n = len(names) // 2
        names = [
            [names[i][r] if (r // width) % 2 == 0 else names[i + n][r] for r in range(8)] for i in range(n)
        ]
    return [names[0].index(i) for i in range(8)]


ROW_OF = row_order()


def save(ustar, coef, ustar_hbm, coef_hbm, sem):
    stores = [
        pltpu.make_async_copy(ustar, ustar_hbm, sem.at[0]),
        pltpu.make_async_copy(coef, coef_hbm, sem.at[1]),
    ]
    for store in stores:
        store.start()
    for store in stores:
        store.wait()


def on_device(phase_mask, pressure, velocity_cot):
    field = pltpu.VMEM((NXL + 2, 48, NZL), F32)
    block = pltpu.VMEM((NXL, NYL, NZL), F32)
    flat = pltpu.VMEM((NXL, NZL), F32)
    flats = pltpu.VMEM((3, NXL, NZL), F32)
    pair = pltpu.VMEM((2, NXL, NZL), F32)
    tile = pltpu.VMEM((8, NZL), F32)
    tiles = pltpu.VMEM((3, 8, NZL), F32)
    dma = pltpu.SemaphoreType.DMA
    in_hbm = pl.BlockSpec(memory_space=pltpu.HBM)
    in_vmem = pl.BlockSpec(memory_space=pltpu.VMEM)
    out_shape = (
        jax.ShapeDtypeStruct((3, NXL, NYL, NZL), F32),
        jax.ShapeDtypeStruct((NXL, NYL, NZL), F32),
    )
    inputs = [
        pltpu.with_memory_space_constraint(a, pltpu.HBM) for a in (phase_mask, pressure, velocity_cot)
    ]
    outs = pl.pallas_call(
        body,
        out_shape=out_shape,
        in_specs=[in_hbm] * 3,
        out_specs=(in_vmem, in_vmem),
        scratch_shapes=[
            pltpu.VMEM((NXL, NYL, NZL), jnp.int32),
            *[field] * 8,
            pltpu.VMEM((NXL + 1, NYL, NZL), F32),
            *[block] * 4,
            pair,
            *[block] * 4,
            pltpu.VMEM((3, 3, NXL, NYL, NZL), F32),
            pltpu.VMEM((4, NXL, NYL, NZL), F32),
            *[pltpu.VMEM((2, 2 * NYL + 8, NZL), F32)] * 2,
            *[pltpu.VMEM((2, 2 * NXL + 8, NZL), F32)] * 2,
            *[tiles] * 3,
            *[pltpu.VMEM((2, NYL, NZL), F32)] * 2,
            *[pair] * 2,
            *[tile] * 3,
            pltpu.VMEM((4, NXL, NZL), F32),
            pltpu.VMEM((4, 8, NZL), F32),
            pltpu.VMEM((4, 8, NZL), F32),
            pltpu.VMEM((4, NXL, NZL), F32),
            *[flat] * 3,
            pltpu.VMEM((2, NYL, NZL), jnp.int32), pltpu.VMEM((NYL, NZL), F32), pair, flat,
            *[flat] * 4,
            *[flats] * 2,
            pltpu.VMEM((3, 2, NXL, NZL), F32),
            pltpu.VMEM((3, 2, NYL, NZL), F32),
            *[tile] * 8,
            pltpu.VMEM((2, 8, NZL), F32),
            *[tiles] * 4,
            pltpu.VMEM((sum(RING ** len(axes) for axes in PHASES), 1, NZL), F32),
            dma((5,)),
            dma((15,)), dma((15,)), dma((3, 6)), dma((3, 6)),
            dma((len(PHASES),)), dma((len(PHASES),)),
            pltpu.SemaphoreType.REGULAR,
            pltpu.SemaphoreType.REGULAR((3, 3)),
            dma((28,)), dma((28,)),
        ],
        compiler_params=pltpu.CompilerParams(
            collective_id=0, has_side_effects=True, vmem_limit_bytes=24 * 1024 * 1024
        ),
        name="projection_adjoint",
    )(*inputs)
    return pl.pallas_call(
        save,
        out_shape=out_shape,
        in_specs=[in_vmem] * 2,
        out_specs=(in_hbm, in_hbm),
        scratch_shapes=[dma((2,))],
        compiler_params=pltpu.CompilerParams(vmem_limit_bytes=4 * 1024 * 1024),
        name="save",
    )(*outs)


def solution(mesh):
    in_specs = (P("gx", "gy", "gz"), P("gx", "gy", "gz"), P(None, "gx", "gy", "gz"))
    out_specs = (P(None, "gx", "gy", "gz"), P("gx", "gy", "gz"))
    return jax.shard_map(
        on_device, mesh=mesh, in_specs=in_specs, out_specs=out_specs, check_vma=False
    )
```
